32 devices in a mesh: blk: 8 (over y, x, core), uly: 4 (over z).
Axes of the slice: x: 2, y: 2, z: 4, core: 2. Of those that a mesh axis runs over, the one named last changes fastest.
Arguments:
- tokens: bfloat16 [4096, 2048], P(('blk', 'uly')), may hold values from -6 to 6
- segment_ids: int32 [4096], P(('blk', 'uly')), may hold values from 0 to 4, as said below
- layer_skip: int32 [5], replicated, may hold values from 0 to 1, as said below
- attn_gain: bfloat16 [2048], P(('blk', 'uly')), may hold values from 0.099609375 to 1.8984375
- w_query: bfloat16 [2048, 2048], P(('blk', 'uly')), may hold values from -0.125 to 0.125
- w_key: bfloat16 [2048, 512], P(('blk', 'uly')), may hold values from -0.125 to 0.125
- w_value: bfloat16 [2048, 512], P(('blk', 'uly')), may hold values from -0.125 to 0.125
- w_output: bfloat16 [2048, 2048], P(None, ('blk', 'uly')), may hold values from -0.5 to 0.5
- mlp_gain: bfloat16 [2048], P(('blk', 'uly')), may hold values from 0.099609375 to 1.8984375
- w_gate: bfloat16 [2048, 5632], P(('blk', 'uly')), may hold values from -0.125 to 0.125
- w_up: bfloat16 [2048, 5632], P(('blk', 'uly')), may hold values from -0.125 to 0.125
- w_down: bfloat16 [5632, 2048], P(None, ('blk', 'uly')), may hold values from -0.078125 to 0.078125
- cotangent: bfloat16 [4096, 2048], P(('blk', 'uly')), may hold values from -6 to 6
Outputs:
- output: bfloat16 [4096, 2048], P(('blk', 'uly'))
- grad_tokens: float32 [4096, 2048], P(('blk', 'uly'))
- grad_attn_gain: float32 [2048], P(('blk', 'uly'))
- grad_query: float32 [2048, 2048], P(('blk', 'uly'))
- grad_key: float32 [2048, 512], P(('blk', 'uly'))
- grad_value: float32 [2048, 512], P(('blk', 'uly'))
- grad_output: float32 [2048, 2048], P(None, ('blk', 'uly'))
- grad_mlp_gain: float32 [2048], P(('blk', 'uly'))
- grad_gate: float32 [2048, 5632], P(('blk', 'uly'))
- grad_up: float32 [2048, 5632], P(('blk', 'uly'))
- grad_down: float32 [5632, 2048], P(None, ('blk', 'uly'))
The draws below stay inside these ranges and needn't reach their ends.
Inputs may be any that keep to these rules, and one draw needn't show every extreme that they name: `segment_ids`: Non-decreasing along the row; every number is used; documents 0 and 1 lie within the first 127 tokens, documents 3 and 4 within the last 127 tokens, and document 2 takes all tokens between them. `layer_skip`: document 2 never skips; exactly one of documents 0 and 1 skips.
All inputs are finite; a program needn't handle non-finite values.
Results may differ from the reference program's by a relative error of at most 0.02.
Values may be sent and summed in bfloat16 or wider, within the bound.
No kernel may reach another device: no remote copies, remote signals or barrier semaphores. Data moves between devices by JAX's collectives and lax.ppermute only.
A program may use at most 384 MiB of HBM per device.

```python
import jax
import jax.numpy as jnp
from jax import lax

D = 2048
HEADS = 16
KV_HEADS = 4
HEAD_DIM = 128
FF = 5632
TOK_DEV = 128
SEQLEN = 4096
N_ULY = 4


def draw_segment_ids(key, part):
    keys = jax.random.split(jax.random.fold_in(key, 11), 4)
    top = (TOK_DEV - 1) // 2 + 1
    head_a = jax.random.randint(keys[0], (), 1, top, dtype=jnp.int32)
    head_b = jax.random.randint(keys[1], (), 1, top, dtype=jnp.int32)
    tail_a = jax.random.randint(keys[2], (), 1, top, dtype=jnp.int32)
    tail_b = jax.random.randint(keys[3], (), 1, top, dtype=jnp.int32)
    places = jnp.arange(SEQLEN, dtype=jnp.int32)
    ids = (places >= head_a).astype(jnp.int32) + (places >= head_a + head_b).astype(jnp.int32) + (places >= SEQLEN - tail_a - tail_b).astype(jnp.int32) + (places >= SEQLEN - tail_b).astype(jnp.int32)
    return ids.astype(jnp.int32)


def draw_layer_skip(key, part):
    keys = jax.random.split(jax.random.fold_in(key, 23), 2)
    pick = jax.random.randint(keys[0], (), 0, 2, dtype=jnp.int32)
    tail = jax.random.randint(keys[1], (2,), 0, 2, dtype=jnp.int32)
    head = jnp.stack([(pick == 0).astype(jnp.int32), (pick == 1).astype(jnp.int32)])
    return jnp.concatenate([head, jnp.zeros((1,), jnp.int32), tail]).astype(jnp.int32)


def with_spikes(drawn, stream_key, source, target, parts, factor):
    def block_of(axis_at):
        return (jnp.arange(drawn.shape[axis_at]) // (drawn.shape[axis_at] // parts)).reshape((-1,) + (1,) * (drawn.ndim - 1 - axis_at))

    near = jax.random.permutation(stream_key, parts)[block_of(target)]
    second = (block_of(target) + parts // 2) % parts
    return jnp.where((block_of(source) == near) | (block_of(source) == second), factor * drawn, drawn)


def block_levels(rng, shape, pieces, least, top_value):
    def one(position, parts):
        steps = jax.random.uniform(jax.random.fold_in(jax.random.fold_in(rng, 6), position), (parts,), jnp.float32, least / len(pieces), top_value / len(pieces))
        return jnp.repeat(jnp.exp(steps), shape[position] // parts).reshape((-1,) + (1,) * (len(shape) - position - 1))

    level = one(*pieces[0])
    for cut in pieces[1:]:
        level = level * one(*cut)
    return level


def centred(key, dims, scale, reach, cuts=(), held_as=jnp.bfloat16):
    loudness = block_levels(key, dims, cuts, -0.22, 0.18) if cuts else 1.0
    values = jax.random.normal(key, dims, jnp.float32) * scale * loudness
    return jnp.minimum(jnp.maximum(values, -reach), reach).astype(held_as)


def noise_with(key, shape, deviation, reach, cuts, heavy, held_as=jnp.bfloat16):
    values = deviation * jax.random.normal(key, shape, jnp.float32)
    if cuts:
        values = values * block_levels(key, shape, cuts, -0.22, 0.18)
    return jnp.clip(with_spikes(values, jax.random.fold_in(key, 3), *heavy), -reach, reach).astype(held_as)


def setup_inputs(seed: int = 0) -> dict:
    splits = jax.random.split(jax.random.key(seed), 14)
    tokens = centred(splits[0], (SEQLEN, D), 1.0, 6.0, ((0, 32),))
    segment_ids = draw_segment_ids(jax.random.fold_in(splits[13], 71), 0)
    layer_skip = draw_layer_skip(jax.random.fold_in(splits[13], 71), 0)
    attn_gain = jnp.clip(1.0 + 0.18 * jax.random.normal(splits[3], (D,), jnp.float32), 0.099609375, 1.8984375).astype(jnp.bfloat16)
    w_query = centred(splits[4], (D, HEADS * HEAD_DIM), D ** -0.5, 0.125, ((0, 32),))
    w_key = centred(splits[5], (D, KV_HEADS * HEAD_DIM), D ** -0.5, 0.125, ((0, 32),))
    w_value = centred(splits[6], (D, KV_HEADS * HEAD_DIM), D ** -0.5, 0.125, ((0, 32),))
    w_output = centred(splits[7], (HEADS * HEAD_DIM, D), (HEADS * HEAD_DIM // 16) ** -0.5, 0.5, ((1, 32),))
    mlp_gain = jnp.clip(1.0 + 0.18 * jax.random.normal(splits[8], (D,), jnp.float32), 0.099609375, 1.8984375).astype(jnp.bfloat16)
    w_gate = centred(splits[9], (D, FF), D ** -0.5, 0.125, ((0, 32),))
    w_up = centred(splits[10], (D, FF), D ** -0.5, 0.125, ((0, 32),))
    w_down = centred(splits[11], (FF, D), FF ** -0.5, 0.078125, ((1, 32),))
    cotangent = noise_with(splits[12], (SEQLEN, D), 1.0, 6.0, ((0, 32),), (0, 1, 32, 2.75))
    return dict(tokens=tokens, segment_ids=segment_ids, layer_skip=layer_skip, attn_gain=attn_gain, w_query=w_query, w_key=w_key, w_value=w_value, w_output=w_output, mlp_gain=mlp_gain, w_gate=w_gate, w_up=w_up, w_down=w_down, cotangent=cotangent)


@jax.custom_vjp
def low(v):
    return lax.optimization_barrier(v.astype(jnp.bfloat16)).astype(jnp.float32)

@jax.custom_vjp
def low_back(v):
    return v

def low_keep(v):
    return (low(v), None)

def low_pass(kept, grad):
    return (grad,)

def back_keep(v):
    return (v, None)

def back_low(kept, grad):
    return (low(grad),)
low.defvjp(low_keep, low_pass)
low_back.defvjp(back_keep, back_low)
EPS = 1e-05
THETA = 10000.0
PRECISE = lax.Precision.HIGHEST

def matmul(left, right):
    return jnp.dot(left, right, precision=PRECISE, preferred_element_type=jnp.float32)

def rms_scale(values):
    return lax.rsqrt(lax.optimization_barrier(jnp.mean(values * values, axis=-1, keepdims=True)) + EPS)

def angle_tables(start, count, head_dim):
    half = head_dim // 2
    spots = (start + lax.iota(jnp.int32, count)).astype(jnp.float32)
    rates = jnp.power(THETA, -lax.iota(jnp.int32, half).astype(jnp.float32) / half)
    angles = spots[:, None] * rates[None, :]
    return (jnp.cos(angles), jnp.sin(angles))

def rotate(values, cosine_table, sine_table):
    half = values.shape[-1] // 2
    first_half = values[..., :half]
    second_half = values[..., half:]
    cosine = cosine_table[:, None, :]
    sine_part = sine_table[:, None, :]
    return jnp.concatenate([first_half * cosine - second_half * sine_part, second_half * cosine + first_half * sine_part], axis=-1)

def attention(query_rot, key_rot, value_low, segments):
    span = N_ULY * TOK_DEV
    share = HEADS // KV_HEADS
    seg_all = segments.astype(jnp.int32)
    spots = lax.iota(jnp.int32, SEQLEN)

    def one_block(index):
        start = (index * span).astype(jnp.int32)
        queries = lax.dynamic_slice_in_dim(query_rot, start, span, 0).reshape(span, KV_HEADS, share, HEAD_DIM)
        query_seg = lax.dynamic_slice_in_dim(seg_all, start, span, 0)
        query_spot = start + lax.iota(jnp.int32, span)
        allowed = (query_seg[:, None] == seg_all[None, :]) & (query_spot[:, None] >= spots[None, :])
        scores = low_back(jnp.einsum('qhgd,khd->qhgk', queries, key_rot, precision=PRECISE) * HEAD_DIM ** (-0.5))
        scores = jnp.where(allowed[:, None, None, :], scores, -1e+30)
        probs = low(jax.nn.softmax(scores, axis=-1))
        attended = jnp.einsum('qhgk,khd->qhgd', probs, value_low, precision=PRECISE)
        return attended.reshape(span, HEADS * HEAD_DIM)
    blocks = lax.map(jax.checkpoint(one_block), lax.iota(jnp.int32, SEQLEN // span))
    return blocks.reshape(SEQLEN, HEADS * HEAD_DIM)

def layer_forward(tokens, attn_gain, w_query, w_key, w_value, w_output, mlp_gain, w_gate, w_up, w_down, keep, segments):
    normed_one = low(tokens * rms_scale(tokens) * attn_gain)
    query = low_back(matmul(normed_one, w_query)).reshape(SEQLEN, HEADS, HEAD_DIM)
    key = low_back(matmul(normed_one, w_key)).reshape(SEQLEN, KV_HEADS, HEAD_DIM)
    value_low = low(low_back(matmul(normed_one, w_value))).reshape(SEQLEN, KV_HEADS, HEAD_DIM)
    cosine_table, sine_table = angle_tables(0, SEQLEN, HEAD_DIM)
    query_rot = low(low_back(rotate(query, cosine_table, sine_table)))
    key_rot = low(low_back(rotate(key, cosine_table, sine_table)))
    attended = low(low_back(attention(query_rot, key_rot, value_low, segments)))
    proj = low_back(matmul(attended, w_output))
    middle = tokens + keep[:, None] * proj
    normed_two = low(middle * rms_scale(middle) * mlp_gain)
    gate = low_back(matmul(normed_two, w_gate))
    up = low_back(matmul(normed_two, w_up))
    hidden = low(jax.nn.silu(gate) * up)
    ffn = low_back(matmul(hidden, w_down))
    return middle + keep[:, None] * ffn

def reference(tokens, segment_ids, layer_skip, attn_gain, w_query, w_key, w_value, w_output, mlp_gain, w_gate, w_up, w_down, cotangent):
    keep = 1.0 - layer_skip[segment_ids].astype(jnp.float32)
    floats = tuple((item.astype(jnp.float32) for item in (tokens, attn_gain, w_query, w_key, w_value, w_output, mlp_gain, w_gate, w_up, w_down)))

    def forward(*params):
        return layer_forward(*params, keep, segment_ids)
    result, pullback = jax.vjp(forward, *floats)
    grads = pullback(cotangent.astype(jnp.float32))
    return (result.astype(jnp.bfloat16), grads[0], grads[1], grads[2], grads[3], grads[4], grads[5], grads[6], grads[7], grads[8], grads[9])
```

```python
import functools

import jax
import jax.numpy as jnp
from jax import lax
from jax.experimental import pallas as pl
from jax.experimental.pallas import tpu as pltpu
from jax.sharding import Mesh
from jax.sharding import PartitionSpec as P

HEADS = 16
KV_HEADS = 4
HEAD_DIM = 128
SHARE = HEADS // KV_HEADS

EPS = 1e-05
THETA = 10000.0
LOG2E = 1.4426950408889634
SCALE = HEAD_DIM ** (-0.5)
FAR = 1e30

AXES = ("far", "x", "core", "zh", "zl")
TEAM = ("x", "zl")

BF = jnp.bfloat16
F32 = jnp.float32


def dot(left, right, left_dim=1, right_dim=0):
    return lax.dot_general(
        left, right, (((left_dim,), (right_dim,)), ((), ())), preferred_element_type=F32
    )


def turned(values, cosine, sine):
    return values * cosine + pltpu.roll(values, HEAD_DIM // 2, axis=1) * sine


def visible(kpos, qpos, qstart):
    return (kpos <= qpos) & (kpos >= qstart)


def is_mixed(starts, base, run):
    mixed = False
    for start in starts:
        inside = (start > base) & (start < base + run)
        mixed = inside if mixed is False else (mixed | inside)
    return mixed


def run_row(meta, sizes, number, run):
    far_n, zh_n = sizes
    far, core, zh = (meta[i] for i in range(3))
    zh_r = lax.rem(number, zh_n)
    core_r = lax.rem(number // zh_n, 2)
    x_r = lax.rem(number // (2 * zh_n), 2)
    far_r = number // (4 * zh_n)
    slot = ((core_r ^ core) * far_n + (far_r ^ far)) * zh_n + (zh_r ^ zh)
    return pl.multiple_of((slot * 2 + x_r) * run, run)


def natural_slot(meta, sizes, i):
    far_n, zh_n = sizes
    far, core, zh = (meta[k] for k in range(3))
    zh_i = i % zh_n if isinstance(i, int) else lax.rem(i, zh_n)
    far_i = i // zh_n % far_n if isinstance(i, int) else lax.rem(i // zh_n, far_n)
    core_i = i // (zh_n * far_n)
    return ((core_i ^ core) * far_n + (far_i ^ far)) * zh_n + (zh_i ^ zh)


def forward_kernel(
    docs, sizes, run, count, meta, q, cosine, sine, qpos, qstart, kown, klocal, *refs
):
    low = meta[3]
    high = low + 2 * sizes[1]
    first = meta[4]
    starts = [meta[5 + d] for d in range(docs)]
    factor = SCALE * LOG2E
    tile = 2 * run
    out, q_rot, lse, kv, sems, vt, vown, top, total, acc = refs[count:]
    copies = load_pieces(refs[:count], kv, sems, 0)
    for copy in copies:
        copy.wait()
    vown[...] = kv[:tile, HEAD_DIM:].T

    def flip(j, _):
        vt[j] = kv[pl.ds(run_row(meta, sizes, j, run), run), HEAD_DIM:].T
        return 0

    lax.fori_loop(first, high, flip, 0)

    heads = range(SHARE)
    keys = kv[:tile, :HEAD_DIM]
    own = visible(kown[...], qpos[...], qstart[...])
    for h in heads:
        lanes = slice(h * HEAD_DIM, (h + 1) * HEAD_DIM)
        q_head = turned(q[:, lanes], cosine[...], sine[...]).astype(BF)
        q_rot[:, lanes] = q_head
        raw = jnp.where(own, dot(keys, q_head, 1, 1), -FAR)
        peak = jnp.max(raw, axis=0, keepdims=True)
        weights = jnp.exp2(raw * factor - peak * factor)
        top[h : h + 1, :] = peak
        total[h : h + 1, :] = jnp.sum(weights, axis=0, keepdims=True)
        acc[h] = dot(vown[...], weights.astype(BF))

    def fold(j, masked):
        base = j * run
        keys = kv[pl.ds(run_row(meta, sizes, j, run), run), :HEAD_DIM]
        values = vt[j]
        seen = (qstart[...] <= base) & (qpos[...] >= base + run - 1)
        if masked:
            allowed = visible(klocal[...] + base, qpos[...], qstart[...])
        for h in heads:
            lanes = slice(h * HEAD_DIM, (h + 1) * HEAD_DIM)
            raw = dot(keys, q_rot[:, lanes], 1, 1)
            before = top[h : h + 1, :]
            if masked:
                raw = jnp.where(allowed, raw, -FAR)
                peak = jnp.maximum(before, jnp.max(raw, axis=0, keepdims=True))
                level = peak * factor
            else:
                new = jnp.max(raw, axis=0, keepdims=True)
                peak = jnp.maximum(before, jnp.where(seen, new, -FAR))
                level = jnp.where(seen, peak * factor, FAR)
            weights = jnp.exp2(raw * factor - level)
            fade = jnp.exp2((before - peak) * factor)
            top[h : h + 1, :] = peak
            total[h : h + 1, :] = total[h : h + 1, :] * fade + jnp.sum(
                weights, axis=0, keepdims=True
            )
            acc[h] = acc[h] * fade + dot(values, weights.astype(BF))

    def step(j, _):
        mixed = is_mixed(starts, j * run, run)
        other = j != low

        @pl.when(other & mixed)
        def _():
            fold(j, True)

        @pl.when(other & jnp.logical_not(mixed))
        def _():
            fold(j, False)

        return 0

    lax.fori_loop(first, high, step, 0)
    for h in heads:
        lanes = slice(h * HEAD_DIM, (h + 1) * HEAD_DIM)
        out[:, lanes] = (acc[h] / total[h : h + 1, :]).T.astype(BF)
    lse[...] = top[...] * factor + jnp.log2(total[...])


def load_natural(meta, sizes, source, target, sems, base):
    slots = 2 * sizes[0] * sizes[1]
    block = source.shape[0] // slots
    copies = []
    for i in range(slots):
        away = pl.ds(pl.multiple_of(natural_slot(meta, sizes, i) * block, block), block)
        copy = pltpu.make_async_copy(
            source.at[away, :], target.at[pl.ds(i * block, block), :], sems.at[base + i]
        )
        copy.start()
        copies.append(copy)
    return copies


def proj_kernel(sizes, meta, attn, w_out, proj, held, sems):
    for copy in load_natural(meta, sizes, w_out, held, sems, 0):
        copy.wait()
    for at in range(0, held.shape[0], 256):
        proj[:, at : at + 256] = dot(attn[...], held[at : at + 256, :], 1, 1).astype(BF)


def backward_kernel(
    docs, sizes, run, count, meta, q, o, g_proj, w_out, lse, cosine, sine, qpos, qstart, kown, klocal, *refs
):
    low = meta[3]
    high = low + 2 * sizes[1]
    first = meta[4]
    starts = [meta[5 + d] for d in range(docs)]
    factor = SCALE * LOG2E
    tile = 2 * run
    grad_q, grad_kv, kv, held, sems, dqt, delta, g = refs[count:]
    copies = load_pieces(refs[:count], kv, sems, 0)
    for copy in load_natural(meta, sizes, w_out, held, sems, count):
        copy.wait()
    total = dot(g_proj[...], held[...])
    for copy in copies:
        copy.wait()
    g[...] = total.astype(BF)
    dqt[...] = jnp.zeros_like(dqt)
    grad_kv[...] = jnp.zeros_like(grad_kv)

    def prepare(h, _):
        lanes = pl.ds(pl.multiple_of(h * HEAD_DIM, HEAD_DIM), HEAD_DIM)
        both = o[:, lanes].astype(F32) * g[:, lanes].astype(F32)
        delta[pl.ds(h, 1), :] = jnp.sum(both.T, axis=0, keepdims=True)
        return 0

    lax.fori_loop(0, SHARE, prepare, 0)

    def key_step(rows, count, kpos, base):
        k_tile = kv[rows, :HEAD_DIM]
        v_tile = kv[rows, HEAD_DIM:]
        kt = k_tile.T

        def head(h, carry):
            grad_k, grad_v = carry
            lanes = slice(h * HEAD_DIM, (h + 1) * HEAD_DIM)
            q_head = q[:, lanes]
            g_head = g[:, lanes]
            raw = dot(k_tile, q_head, 1, 1) * factor
            level = lse[h : h + 1, :]
            if kpos is not None:
                probs = jnp.exp2(raw - level)
                probs = jnp.where(visible(kpos, qpos[...], qstart[...]), probs, 0.0)
            else:
                seen = (qstart[...] <= base) & (qpos[...] >= base + run - 1)
                probs = jnp.exp2(raw - jnp.where(seen, level, FAR))
            slopes = dot(v_tile, g_head, 1, 1)
            grads = (probs * (slopes - delta[h : h + 1, :])).astype(BF)
            grad_v = grad_v + dot(probs.astype(BF), g_head)
            grad_k = grad_k + dot(grads, q_head)
            dqt[h] = dqt[h] + dot(kt, grads)
            return grad_k, grad_v

        zero = jnp.zeros((count, HEAD_DIM), F32)
        grad_k, grad_v = zero, zero
        for h in range(SHARE):
            grad_k, grad_v = head(h, (grad_k, grad_v))
        grad_kv[rows, :HEAD_DIM] = (grad_k * SCALE).astype(BF)
        grad_kv[rows, HEAD_DIM:] = grad_v.astype(BF)

    key_step(pl.ds(0, tile), tile, kown[...], 0)

    def step(j, _):
        base = j * run
        mixed = is_mixed(starts, base, run)
        other = j != low
        rows = pl.ds(run_row(meta, sizes, j, run), run)

        @pl.when(other & mixed)
        def _():
            key_step(rows, run, klocal[...] + base, base)

        @pl.when(other & jnp.logical_not(mixed))
        def _():
            key_step(rows, run, None, base)

        return 0

    lax.fori_loop(first, high, step, 0)

    def finish(h, _):
        lanes = pl.ds(pl.multiple_of(h * HEAD_DIM, HEAD_DIM), HEAD_DIM)
        rotated = (dqt[h] * SCALE).T.astype(BF).astype(F32)
        grad_q[:, lanes] = turned(rotated, cosine[...], -sine[...]).astype(BF)
        return 0

    lax.fori_loop(0, SHARE, finish, 0)


SMEM = pl.BlockSpec(memory_space=pltpu.SMEM)
VMEM = pl.BlockSpec(memory_space=pltpu.VMEM)
ANY = pl.BlockSpec(memory_space=pl.ANY)


def attention_forward(meta, docs, sizes, q, tables, kv):
    tile = q.shape[0]
    run = tile // 2
    span = sum(a.shape[0] for a in kv)
    pairs = tile * span // 2 * SHARE
    return pl.pallas_call(
        functools.partial(forward_kernel, docs, sizes, run, len(kv)),
        out_shape=(
            jax.ShapeDtypeStruct(q.shape, BF),
            jax.ShapeDtypeStruct(q.shape, BF),
            jax.ShapeDtypeStruct((SHARE, tile), F32),
        ),
        in_specs=[SMEM] + [VMEM] * (1 + len(tables)) + [ANY] * len(kv),
        out_specs=(VMEM, VMEM, VMEM),
        scratch_shapes=[
            pltpu.VMEM((span, 2 * HEAD_DIM), BF),
            pltpu.SemaphoreType.DMA((len(kv),)),
            pltpu.VMEM((span // run, HEAD_DIM, run), BF),
            pltpu.VMEM((HEAD_DIM, tile), BF),
            pltpu.VMEM((SHARE, tile), F32),
            pltpu.VMEM((SHARE, tile), F32),
            pltpu.VMEM((SHARE, HEAD_DIM, tile), F32),
        ],
        compiler_params=pltpu.CompilerParams(vmem_limit_bytes=56 << 20),
        cost_estimate=pl.CostEstimate(
            flops=pairs * HEAD_DIM * 4, bytes_accessed=4 << 20, transcendentals=pairs
        ),
        name="attention_forward",
    )(meta, q, *tables, *kv)


def attention_backward(meta, docs, sizes, q, o, g_proj, w_out, lse, tables, kv):
    tile = q.shape[0]
    run = tile // 2
    span = sum(a.shape[0] for a in kv)
    pairs = tile * span // 2 * SHARE
    return pl.pallas_call(
        functools.partial(backward_kernel, docs, sizes, run, len(kv)),
        out_shape=(
            jax.ShapeDtypeStruct(q.shape, BF),
            jax.ShapeDtypeStruct((span, 2 * HEAD_DIM), BF),
        ),
        in_specs=[SMEM, VMEM, VMEM, VMEM, ANY] + [VMEM] * (1 + len(tables)) + [ANY] * len(kv),
        out_specs=(VMEM, VMEM),
        scratch_shapes=[
            pltpu.VMEM((span, 2 * HEAD_DIM), BF),
            pltpu.VMEM(w_out.shape, BF),
            pltpu.SemaphoreType.DMA((len(kv) + 2 * sizes[0] * sizes[1],)),
            pltpu.VMEM((SHARE, HEAD_DIM, tile), F32),
            pltpu.VMEM((SHARE, tile), F32),
            pltpu.VMEM(q.shape, BF),
        ],
        compiler_params=pltpu.CompilerParams(vmem_limit_bytes=56 << 20),
        cost_estimate=pl.CostEstimate(
            flops=pairs * HEAD_DIM * 10, bytes_accessed=6 << 20, transcendentals=pairs
        ),
        name="attention_backward",
    )(meta, q, o, g_proj, w_out, lse, *tables, *kv)


def call(kernel, name, shapes, operands, specs=None, scratch=(), flops=1 << 20):
    nbytes = sum(a.size * a.dtype.itemsize for a in operands)
    return pl.pallas_call(
        kernel,
        out_shape=tuple(jax.ShapeDtypeStruct(s, d) for s, d in shapes),
        in_specs=specs or [VMEM] * len(operands),
        out_specs=(VMEM,) * len(shapes),
        scratch_shapes=list(scratch),
        compiler_params=pltpu.CompilerParams(vmem_limit_bytes=56 << 20),
        cost_estimate=pl.CostEstimate(flops=flops, bytes_accessed=nbytes, transcendentals=0),
        name=name,
    )(*operands)


def load_pieces(pieces, target, sems, base):
    copies = []
    place = 0
    for i, piece in enumerate(pieces):
        rows = piece.shape[0]
        copy = pltpu.make_async_copy(piece, target.at[pl.ds(place, rows), :], sems.at[base + i])
        copy.start()
        copies.append(copy)
        place += rows
    return copies


def pack_kernel(team, count, *refs):
    out = refs[count]
    place = 0
    for shard in refs[:count]:
        part = shard.shape[1] // team
        for t in range(team):
            out[t, :, place : place + part] = shard[:, t * part : (t + 1) * part]
        place += part


def pack(team, shards):
    width = sum(s.shape[1] for s in shards) // team
    kernel = functools.partial(pack_kernel, team, len(shards))
    return call(kernel, "pack", [((team, shards[0].shape[0], width), BF)], shards)[0]


def slots_kernel(chunk, scaled, copies, order, array, keep, own, sent):
    width = array.shape[1]
    for j in range(width // chunk):
        if chunk < width:
            block = array[:, pl.ds(pl.multiple_of(order[j] * chunk, chunk), chunk)]
        else:
            block = array[...]
        lanes = pl.ds(j * chunk, chunk)
        own[:, lanes] = block
        if scaled:
            block = (block.astype(F32) * keep[...]).astype(BF)
        for t in range(copies):
            sent[t, :, lanes] = block


def slots_and_copies(array, keep, scaled, copies):
    chunk, order = slot_order(array.shape[1], True)
    if order is None:
        array, order = to_slots(array), jnp.zeros((1,), jnp.int32)
    kernel = functools.partial(slots_kernel, chunk, scaled, copies)
    shapes = [(array.shape, BF), ((copies,) + array.shape, BF)]
    return call(kernel, "to_slots", shapes, [order, array, keep], [SMEM, VMEM, VMEM])


def natural_kernel(chunk, order, array, out):
    for j in range(array.shape[1] // chunk):
        out[:, j * chunk : (j + 1) * chunk] = array[
            :, pl.ds(pl.multiple_of(order[j] * chunk, chunk), chunk)
        ]


def to_natural(array):
    chunk, order = slot_order(array.shape[1], False)
    if order is None:
        return from_slots(array)
    kernel = functools.partial(natural_kernel, chunk)
    return call(kernel, "from_slots", [(array.shape, array.dtype)], [order, array], [SMEM, VMEM])[0]


def slot_order(width, forward):
    far_n, x_n, core_n, zh_n, _ = [lax.axis_size(a) for a in AXES]
    far, _, core, zh, _ = [lax.axis_index(a) for a in AXES]
    count = far_n * x_n * core_n * zh_n
    chunk = width // count
    if chunk % HEAD_DIM:
        return width, None
    j = lax.iota(jnp.int32, count)
    if forward:
        c, f, z, x = j // (far_n * zh_n * x_n), j // (zh_n * x_n) % far_n, j // x_n % zh_n, j % x_n
        return chunk, (((f ^ far) * x_n + x) * core_n + (c ^ core)) * zh_n + (z ^ zh)
    f, x, c, z = j // (x_n * core_n * zh_n), j // (core_n * zh_n) % x_n, j // zh_n % core_n, j % zh_n
    return chunk, (((c ^ core) * far_n + (f ^ far)) * zh_n + (z ^ zh)) * x_n + x


def project_kernel(count, ids, x, cosine, sine, *refs):
    pieces = refs[:count]
    normed, scale, q, kv, small, w, sems = refs[count:]
    copies = load_pieces(pieces, w, sems, 0)
    rows = x.shape[0]
    features = x.shape[1]
    step = 128

    def squares(i, _):
        at = pl.ds(pl.multiple_of(i * step, step), step)
        block = x[at, :].astype(F32)
        scale[at, :] = lax.rsqrt(jnp.sum(block * block, axis=1, keepdims=True) / features + EPS)
        return 0

    lax.fori_loop(0, rows // step, squares, 0)
    for copy in copies:
        copy.wait()
    width = w.shape[1] - HEAD_DIM
    turned_small = w[:, width:].astype(F32).T
    small[...] = turned_small[: small.shape[0], :]
    gain = small[ids : ids + 1, :]

    def norm(i, _):
        at = pl.ds(pl.multiple_of(i * step, step), step)
        normed[at, :] = (x[at, :].astype(F32) * scale[at, :] * gain).astype(BF)
        return 0

    lax.fori_loop(0, rows // step, norm, 0)
    for at in range(0, width - 2 * HEAD_DIM, 256):
        q[:, at : at + 256] = dot(normed[...], w[:, at : at + 256])
    both = dot(normed[...], w[:, width - 2 * HEAD_DIM : width])
    kv[:, :HEAD_DIM] = turned(both[:, :HEAD_DIM], cosine[...], sine[...]).astype(BF)
    kv[:, HEAD_DIM:] = both[:, HEAD_DIM:].astype(BF)


def project(tokens_all, cosine, sine, pieces, ids):
    rows, features = tokens_all.shape
    width = pieces[0].shape[1]
    held = -(-(ids + 2) // 8) * 8
    return call(
        functools.partial(project_kernel, len(pieces), ids),
        "project",
        [
            ((rows, features), BF),
            ((rows, 1), F32),
            ((rows, width - 3 * HEAD_DIM), F32),
            ((rows, 2 * HEAD_DIM), BF),
            ((held, features), F32),
        ],
        [tokens_all, cosine, sine, *pieces],
        [VMEM] * 3 + [ANY] * len(pieces),
        [pltpu.VMEM((features, width), BF), pltpu.SemaphoreType.DMA((len(pieces),))],
        2 * rows * features * width,
    )


def middle_kernel(parts, tokens, keep, gain, middle, sent):
    proj = total_of([parts[t] for t in range(parts.shape[0])])
    mid = tokens[...].astype(F32) + keep[...] * proj
    scale = lax.rsqrt(jnp.mean(mid * mid, axis=1, keepdims=True) + EPS)
    middle[...] = mid
    normed = (mid * scale * gain[...]).astype(BF)
    for t in range(sent.shape[0]):
        sent[t] = normed


def middle_grad_kernel(parts, middle, cotangent, keep, gain, grad_middle, sent, terms):
    grad = total_of([parts[t] for t in range(parts.shape[0])])
    mid = middle[...]
    scale = lax.rsqrt(jnp.mean(mid * mid, axis=1, keepdims=True) + EPS)
    gained = grad * gain[...]
    terms[...] = (grad * mid * scale).astype(BF)
    result = (
        cotangent[...].astype(F32)
        + scale * gained
        - mid * scale**3 * jnp.mean(gained * mid, axis=1, keepdims=True)
    )
    grad_middle[...] = result
    proj = (keep[...] * result).astype(BF)
    for t in range(sent.shape[0]):
        sent[t] = proj


def token_grad_kernel(parts, tokens, grad_middle, gain, out):
    grad = total_of([parts[t] for t in range(parts.shape[0])])
    x = tokens[...].astype(F32)
    scale = lax.rsqrt(jnp.mean(x * x, axis=1, keepdims=True) + EPS)
    gained = grad * gain[...]
    out[...] = (
        grad_middle[...]
        + scale * gained
        - x * scale**3 * jnp.mean(gained * x, axis=1, keepdims=True)
    )


def output_kernel(parts, middle, keep, out):
    ffn = total_of([parts[t] for t in range(parts.shape[0])])
    out[...] = (middle[...] + keep[...] * ffn).astype(BF)


def mlp_kernel(sizes, counts, meta, x, g, *refs):
    total = sum(counts)
    gate_pieces, up_pieces = refs[: counts[0]], refs[counts[0] : total]
    down = refs[total]
    hidden, grad_gate, grad_up, grad_x, ffn, w_g, w_u, w_d, sems = refs[total + 1 :]
    copies = load_pieces(gate_pieces, w_g, sems, 0)
    copies += load_pieces(up_pieces, w_u, sems, counts[0])
    late = load_natural(meta, sizes, down, w_d, sems, total)
    for copy in copies:
        copy.wait()
    features, width = w_g.shape

    def columns(lanes, wait=()):
        gate = dot(x[...], w_g[:, lanes])
        up = dot(x[...], w_u[:, lanes])
        for copy in wait:
            copy.wait()
        grad = dot(g[...], w_d[:, lanes])
        sig = 1.0 / (1.0 + jnp.exp(-gate))
        silu = gate * sig
        hidden[:, lanes] = (silu * up).astype(BF)
        grad_gate[:, lanes] = (grad * up * sig * (1.0 + gate * (1.0 - sig))).astype(BF)
        grad_up[:, lanes] = (grad * silu).astype(BF)

    step = 256
    tail = width % step
    columns(pl.ds(width - tail, tail) if tail else pl.ds(width - step, step), late)

    def chunk(i, _):
        columns(pl.ds(pl.multiple_of(i * step, step), step))
        return 0

    lax.fori_loop(0, (width - 1) // step, chunk, 0)

    def back_rows(i, _):
        at = pl.ds(pl.multiple_of(i * step, step), step)
        total = dot(grad_gate[...], w_g[at, :], 1, 1) + dot(grad_up[...], w_u[at, :], 1, 1)
        grad_x[:, at] = total.astype(BF)
        ffn[:, at] = dot(hidden[...], w_d[at, :], 1, 1).astype(BF)
        return 0

    lax.fori_loop(0, features // step, back_rows, 0)


def mlp(meta, sizes, x, g, w_gate, w_up, w_down):
    rows, features = x.shape
    width = w_down.shape[1]
    counts = (len(w_gate), len(w_up))
    pieces = [*w_gate, *w_up, w_down]
    return call(
        functools.partial(mlp_kernel, sizes, counts),
        "mlp",
        [((rows, width), BF)] * 3 + [((rows, features), BF)] * 2,
        [meta, x, g, *pieces],
        [SMEM] + [VMEM] * 2 + [ANY] * len(pieces),
        [
            *([pltpu.VMEM((features, width), BF)] * 3),
            pltpu.SemaphoreType.DMA((sum(counts) + 2 * sizes[0] * sizes[1],)),
        ],
        12 * rows * features * width,
    )


def outer_kernel(meta, left, right, *refs):
    product = dot(left[...].T, right[...])
    if len(refs) == 2:
        product = product + refs[0][...].astype(F32)
    refs[-1][...] = product.astype(BF)


def outer(meta, sizes, left, right, half=None, natural=False, added=None):
    features = left.shape[1]
    if features // (2 * sizes[0] * sizes[1]) % HEAD_DIM:
        sizes_held = features if half is None else features // 2
        part = left if half is None else left[:, half * sizes_held : (half + 1) * sizes_held]
        product = dot(part, right, 0, 0)
        if natural:
            shape = (2, sizes[0], sizes[1], -1, right.shape[1])
            product = product.reshape(shape)
            for axis, name in enumerate(("core", "far", "zh")):
                product = by_distance(product, axis, lax.axis_index(name))
            product = product.reshape(features, -1)
        return (product if added is None else product + added.astype(F32)).astype(BF)
    slots = 2 * sizes[0] * sizes[1]
    rows, block, width = left.shape[0], features // slots, right.shape[1]
    count, start = (slots, 0) if half is None else (slots // 2, half * slots // 2)
    held = pl.BlockSpec((block, width), lambda i, m: (i, 0))
    return pl.pallas_call(
        outer_kernel,
        out_shape=jax.ShapeDtypeStruct((count * block, width), BF),
        grid_spec=pltpu.PrefetchScalarGridSpec(
            num_scalar_prefetch=1,
            grid=(count,),
            in_specs=[
                pl.BlockSpec((rows, block), lambda i, m: (0, start + i)),
                pl.BlockSpec((rows, width), lambda i, m: (0, 0)),
            ]
            + ([] if added is None else [held]),
            out_specs=pl.BlockSpec((block, width), lambda i, m: (natural_slot(m, sizes, i), 0))
            if natural
            else held,
        ),
        compiler_params=pltpu.CompilerParams(vmem_limit_bytes=48 << 20),
        cost_estimate=pl.CostEstimate(
            flops=2 * rows * count * block * width,
            bytes_accessed=2 * count * block * (rows + width),
            transcendentals=0,
        ),
        name="outer",
    )(meta, left, right, *([] if added is None else [added]))


def qkv_grad_kernel(count, grad_q, grad_kv, x, scale, *refs):
    pieces = refs[:count]
    out, terms, w, sems = refs[count:]
    for copy in load_pieces(pieces, w, sems, 0):
        copy.wait()
    q_width = grad_q.shape[1]
    step = 256

    def rows_of(i, _):
        at = pl.ds(pl.multiple_of(i * step, step), step)
        grad = dot(grad_q[...], w[at, :q_width], 1, 1) + dot(
            grad_kv[...], w[at, q_width : q_width + 2 * HEAD_DIM], 1, 1
        )
        out[:, at] = grad.astype(BF)
        terms[:, at] = (grad * x[:, at].astype(F32) * scale[...]).astype(BF)
        return 0

    lax.fori_loop(0, w.shape[0] // step, rows_of, 0)


def qkv_grad(grad_q, grad_kv, tokens_all, scale_all, pieces):
    rows, features = tokens_all.shape
    width = pieces[0].shape[1]
    return call(
        functools.partial(qkv_grad_kernel, len(pieces)),
        "qkv_grad",
        [((rows, features), BF)] * 2,
        [grad_q, grad_kv, tokens_all, scale_all, *pieces],
        [VMEM] * 4 + [ANY] * len(pieces),
        [pltpu.VMEM((features, width), BF), pltpu.SemaphoreType.DMA((len(pieces),))],
        2 * rows * features * width,
    )


def after(value, *done):
    return lax.optimization_barrier((value, done))[0]


def together(*values):
    return lax.optimization_barrier(values)


def swap(block, axes, distance):
    size = lax.axis_size(axes)
    return lax.ppermute(block, axes, [(i, i ^ distance) for i in range(size)])


def by_distance(array, axis, index):
    size = array.shape[axis]
    bit = 1
    while bit < size:
        shape = array.shape[:axis] + (size // (2 * bit), 2, bit) + array.shape[axis + 1 :]
        pairs = array.reshape(shape)
        flipped = jnp.flip(pairs, axis + 1)
        array = jnp.where((index & bit) != 0, flipped, pairs).reshape(array.shape)
        bit *= 2
    return array


def halves(array):
    half = array.shape[1] // 2
    return array[:, :half], array[:, half:]


def to_team(pieces):
    return lax.all_to_all(pieces, TEAM, split_axis=0, concat_axis=0, tiled=True)


def sum_team(partial):
    team = lax.axis_size(TEAM)
    return to_team(partial.reshape(team, partial.shape[0] // team, partial.shape[1]))


def total_of(parts):
    total = parts[0].astype(F32)
    for i in range(1, len(parts)):
        total = total + parts[i].astype(F32)
    return total


def plane_direct(block):
    size = lax.axis_size("far") * lax.axis_size("zh")
    return [block] + [swap(block, ("far", "zh"), d) for d in range(1, size)]


def plane_first(block):
    near = [swap(block, "zh", d) for d in range(1, lax.axis_size("zh"))]
    far = [[swap(block, "far", d)] for d in range(1, lax.axis_size("far"))]
    return block, near, far


def plane_second(first, *done):
    block, near, far = first
    if done:
        near = after(near, *done)
    far = [f + [swap(b, "far", d + 1) for b in near] for d, f in enumerate(far)]
    return sum(far, [block] + near)


def both_cores(plane):
    if len(plane) > 4:
        plane = [jnp.concatenate(plane, axis=0)]
    return list(plane) + [swap(b, "core", 1) for b in plane]


def sum_axis(part, axis, *done):
    size = lax.axis_size(axis)
    rows = part.shape[0] // size
    got = [swap(part[d * rows : (d + 1) * rows], axis, d) for d in range(1, size)]
    if done:
        got = after(got, *done)
    return total_of([part[:rows]] + got).astype(BF)


SLOT = ("core", "far", "zh")


def spread(block):
    return lax.all_gather(block, SLOT, axis=0, tiled=True)


def gather_back(partial):
    return lax.psum_scatter(partial, SLOT, scatter_dimension=0, tiled=True)


def to_owner(part):
    team = lax.axis_size(TEAM)
    return to_team(part.reshape(team, part.shape[0] // team, part.shape[1]))


def wide(pieces):
    return pieces.transpose(1, 0, 2).reshape(pieces.shape[1], -1).astype(F32)


def turn(values, cosine, sine):
    half = HEAD_DIM // 2
    other = jnp.concatenate([values[:, half:], values[:, :half]], axis=1)
    return values * cosine + other * sine


def to_slots(array):
    sizes = [lax.axis_size(a) for a in AXES]
    rows, width = array.shape
    grid = array.reshape(rows, *sizes[:4], width // (sizes[0] * sizes[1] * sizes[2] * sizes[3]))
    for axis in (0, 2, 3):
        grid = by_distance(grid, axis + 1, lax.axis_index(AXES[axis]))
    return grid.transpose(0, 3, 1, 4, 2, 5).reshape(rows, width)


def from_slots(array):
    far, x, core, zh, zl = [lax.axis_size(a) for a in AXES]
    rows, width = array.shape
    grid = array.reshape(rows, core, far, zh, x, width // (core * far * zh * x))
    grid = grid.transpose(0, 2, 4, 1, 3, 5)
    for axis in (0, 2, 3):
        grid = by_distance(grid, axis + 1, lax.axis_index(AXES[axis]))
    return grid.reshape(rows, width)


def per_device(
    tokens,
    segment_ids,
    layer_skip,
    attn_gain,
    w_query,
    w_key,
    w_value,
    w_output,
    mlp_gain,
    w_gate,
    w_up,
    w_down,
    cotangent,
):
    far_n, x_n, core_n, zh_n, zl_n = [lax.axis_size(a) for a in AXES]
    far, x, core, zh, zl = [lax.axis_index(a) for a in AXES]
    team = x_n * zl_n
    rows = tokens.shape[0]
    tile = team * rows
    run = zl_n * rows
    docs = layer_skip.shape[0]
    part = HEADS * HEAD_DIM // team
    ff = w_gate.shape[1] // team
    width = attn_gain.shape[0]
    features = tokens.shape[1]

    ids = rows // width
    doc_index = lax.iota(jnp.int32, docs)
    skipped = jnp.sum(
        jnp.where(segment_ids[:, None] == doc_index[None, :], layer_skip[None, :], 0), axis=1
    )
    keep = (1 - skipped).astype(F32)[:, None]
    small = jnp.concatenate(
        [segment_ids.astype(BF).reshape(width, ids), attn_gain[:, None], mlp_gain[:, None]], axis=1
    )
    small = jnp.pad(small, ((0, 0), (0, HEAD_DIM - ids - 2)))
    small = jnp.concatenate([small] * team, axis=1)
    first_rows = to_team(pack(team, [w_query, w_key, w_value, small, w_gate]))
    first_rows = first_rows.reshape(-1, first_rows.shape[2])
    qkv_width = part + 3 * HEAD_DIM
    qkv_plane = plane_first(first_rows[:, :qkv_width])
    gate_rows = first_rows[:, qkv_width:]

    last_rows = pack(team, [w_output.T, w_up, w_down.T])
    tokens_own, tokens_sent = slots_and_copies(tokens, keep, False, team)
    cot_own, cot_sent = slots_and_copies(cotangent, keep, True, team)
    tokens_all = to_team(after(tokens_sent, first_rows)).reshape(tile, features)

    local = lax.iota(jnp.int32, tile)
    place = (local // run) * (core_n * zh_n * run) + local % run
    position = ((far * x_n * core_n + core) * zh_n + zh) * run + place
    rates = jnp.power(THETA, -lax.iota(jnp.int32, HEAD_DIM // 2).astype(F32) / (HEAD_DIM // 2))
    angles = position.astype(F32)[:, None] * rates[None, :]
    cosine = jnp.cos(angles)
    sine = jnp.sin(angles)
    cosine = jnp.concatenate([cosine, cosine], axis=1)
    sine = jnp.concatenate([-sine, sine], axis=1)

    qkv_near, last_rows, cot_sent = together(qkv_plane[1], last_rows, cot_sent)
    qkv_plane = (qkv_plane[0], qkv_near, qkv_plane[2])
    gate_plane = plane_first(gate_rows)
    w_qkv = both_cores(plane_second(qkv_plane))
    last_rows = to_team(after(last_rows, tokens_all)).reshape(-1, last_rows.shape[2])
    tokens_all, gate_plane, w_qkv, cosine, sine, last_rows = together(
        tokens_all, gate_plane, w_qkv, cosine, sine, last_rows
    )
    gate_plane = plane_second(gate_plane)
    w_out = spread(last_rows[:, :part])
    grad_ffn = to_team(after(cot_sent, last_rows))

    normed_one, scale_all, q, kv, small_all = project(tokens_all, cosine, sine, w_qkv, ids)
    kv_plane = plane_first(kv)
    gain_one = small_all[ids : ids + 1]
    gain_two = small_all[ids + 1 : ids + 2]
    doc_starts = jnp.sum(
        (small_all[None, :ids] < doc_index.astype(F32)[:, None, None]).astype(F32), axis=(1, 2)
    ).astype(jnp.int32)
    query_seg = jnp.sum((position[:, None] >= doc_starts[None, 1:]).astype(jnp.int32), axis=1)
    query_start = jnp.sum(
        jnp.where(query_seg[:, None] == doc_index[None, :], doc_starts[None, :], 0), axis=1
    )
    low = (far * x_n * core_n + core) * zh_n + zh
    first_start = jnp.max(jnp.where(doc_starts <= low * run, doc_starts, 0))
    meta = jnp.concatenate([jnp.stack([far, core, zh, low, first_start // run]), doc_starts])
    sizes = (far_n, zh_n)
    tables = (
        cosine,
        sine,
        position[None, :],
        query_start[None, :],
        position[:, None],
        lax.iota(jnp.int32, run)[:, None],
    )
    kv_plane, meta, tables = together(kv_plane, meta, tables)
    kv_plane = plane_second(kv_plane)
    kv_plane, gate_plane, last_rows, grad_ffn = together(
        kv_plane, gate_plane, last_rows, grad_ffn
    )
    w_d = spread(last_rows[:, part + ff :])
    kv = both_cores(kv_plane)
    up_plane = plane_first(last_rows[:, part : part + ff])
    attn, query, log_total = attention_forward(meta, docs, sizes, q, tables, kv)
    attn, up_plane = together(attn, up_plane)
    grad_ffn = grad_ffn.reshape(tile, features)

    proj = call(
        functools.partial(proj_kernel, sizes),
        "proj",
        [((tile, features), BF)],
        [meta, attn, w_out],
        [SMEM, VMEM, ANY],
        [pltpu.VMEM(w_out.shape, BF), pltpu.SemaphoreType.DMA((2 * far_n * zh_n,))],
    )[0]
    gate_plane = after(gate_plane, attn)
    proj = sum_team(proj)
    up_plane = plane_second(up_plane)
    w_g = both_cores(gate_plane)
    proj, up_plane, w_g = together(proj, up_plane, w_g)
    middle, normed_sent = call(
        middle_kernel,
        "middle",
        [((rows, features), F32), ((team, rows, features), BF)],
        [proj, tokens_own, keep, gain_two],
    )
    normed_two = to_team(normed_sent)
    w_u = both_cores(up_plane)
    normed_two, w_u = together(normed_two, w_u)
    normed_two = normed_two.reshape(tile, features)

    hidden, grad_gate_act, grad_up_act, grad_two, ffn = mlp(
        meta, sizes, normed_two, grad_ffn, w_g, w_u, w_d
    )
    grad_two_parts = sum_team(grad_two)
    grad_down = outer(meta, sizes, grad_ffn, hidden, natural=True)
    other_up = swap(outer(meta, sizes, normed_two, grad_up_act, half=1), "core", 1)
    grad_gate = outer(meta, sizes, normed_two, grad_gate_act, natural=True)
    up_core = outer(meta, sizes, normed_two, grad_up_act, half=0, added=other_up)
    grad_two_parts, up_core, grad_gate = together(grad_two_parts, up_core, grad_gate)
    grad_down = gather_back(grad_down)
    grad_gate = gather_back(grad_gate)
    grad_middle, grad_proj_sent, terms_two = call(
        middle_grad_kernel,
        "middle_grad",
        [((rows, features), F32), ((team, rows, features), BF), ((rows, features), BF)],
        [grad_two_parts, middle, cot_own, keep, gain_two],
    )
    grad_proj = to_team(grad_proj_sent)
    grad_proj = grad_proj.reshape(tile, features)
    ffn = sum_team(after(ffn, grad_proj))
    grad_query, grad_kv = attention_backward(
        meta, docs, sizes, query, attn, grad_proj, w_out, log_total, tables, kv
    )
    up_far = sum_axis(up_core, "far", grad_kv)
    grad_query, grad_kv, ffn, up_far = together(grad_query, grad_kv, ffn, up_far)
    half = grad_kv.shape[0] // 2
    other_kv = swap(grad_kv[half:], "core", 1)
    grad_kv = grad_kv[:half].astype(F32) + other_kv.astype(F32)
    grad_kv_parts = [grad_kv[:tile]] + [
        swap(grad_kv[d * tile : (d + 1) * tile].astype(BF), ("far", "zh"), d)
        for d in range(1, far_n * zh_n)
    ]
    output = to_natural(
        call(output_kernel, "output", [((rows, features), BF)], [ffn, middle, keep])[0]
    )
    other_q = jnp.concatenate(
        [
            outer(meta, sizes, normed_one, grad_query, half=1),
            outer(meta, sizes, grad_proj, attn, half=1),
        ],
        axis=1,
    )
    other_q = swap(other_q, "core", 1)
    own_q = jnp.concatenate(
        [
            outer(meta, sizes, normed_one, grad_query, half=0),
            outer(meta, sizes, grad_proj, attn, half=0),
        ],
        axis=1,
    )
    q_core = (own_q.astype(F32) + other_q.astype(F32)).astype(BF)
    grad_kv_parts, q_core = together(grad_kv_parts, q_core)
    q_far = sum_axis(q_core, "far")
    up_zh = sum_axis(up_far, "zh")
    grad_kv_sum = total_of(grad_kv_parts)
    grad_key = turn(grad_kv_sum[:, :HEAD_DIM].astype(BF).astype(F32), cosine, -sine).astype(BF)
    grad_kv_tok = jnp.concatenate([grad_key, grad_kv_sum[:, HEAD_DIM:].astype(BF)], axis=1)
    grad_one, terms_one = qkv_grad(grad_query, grad_kv_tok, tokens_all, scale_all, w_qkv)
    grad_one = sum_team(grad_one)

    lanes = lax.broadcasted_iota(jnp.int32, (tile + rows, HEAD_DIM), 1)
    which = lax.broadcasted_iota(jnp.int32, (tile + rows, HEAD_DIM), 0) // tile
    pick = (lanes == which).astype(BF)
    terms = jnp.concatenate([terms_one, terms_two], axis=0)
    other_small, own_small = [
        jnp.concatenate(
            [
                outer(meta, sizes, normed_one, grad_kv_tok, half=i),
                outer(meta, sizes, terms, pick, half=i),
            ],
            axis=1,
        )
        for i in (1, 0)
    ]
    other_small = swap(other_small, "core", 1)
    small_core = (own_small.astype(F32) + other_small.astype(F32)).astype(BF)
    grad_one, small_core, q_far, up_zh = together(grad_one, small_core, q_far, up_zh)
    q_zh = sum_axis(q_far, "zh")
    rows_held = small_core.shape[0] // (far_n * zh_n)
    small_sum = total_of(
        [small_core[:rows_held]]
        + [
            swap(small_core[d * rows_held : (d + 1) * rows_held], ("far", "zh"), d)
            for d in range(1, far_n * zh_n)
        ]
    ).astype(BF)
    grad_up, grad_down, grad_gate = [to_owner(a) for a in (up_zh, grad_down, grad_gate)]
    grad_w = to_owner(jnp.concatenate([q_zh, small_sum], axis=1))
    grad_out = grad_w[:, :, part : 2 * part]
    grad_w = jnp.concatenate([grad_w[:, :, :part], grad_w[:, :, 2 * part :]], axis=2)
    gains = total_of(grad_w[:, :, part + 2 * HEAD_DIM :])
    grad_tokens = to_natural(
        call(
            token_grad_kernel,
            "token_grad",
            [((rows, features), F32)],
            [grad_one, tokens_own, grad_middle, gain_one],
        )[0]
    )
    return (
        output,
        grad_tokens,
        gains[:, 0],
        wide(grad_w[:, :, :part]),
        wide(grad_w[:, :, part : part + HEAD_DIM]),
        wide(grad_w[:, :, part + HEAD_DIM : part + 2 * HEAD_DIM]),
        wide(grad_out).T,
        gains[:, 1],
        wide(grad_gate),
        wide(grad_up),
        wide(grad_down).T,
    )


def solution(mesh):
    blk, uly = mesh.shape["blk"], mesh.shape["uly"]
    grid = Mesh(mesh.devices.reshape(blk // 4, 2, 2, uly // 2, 2), AXES)
    rows = P(AXES, None)
    cols = P(None, AXES)
    flat = P(AXES)
    return jax.shard_map(
        per_device,
        mesh=grid,
        in_specs=(
            rows, flat, P(), flat, rows, rows, rows, cols, flat, rows, rows, cols, rows,
        ),
        out_specs=(rows, rows, flat, rows, rows, rows, cols, flat, rows, rows, cols),
        check_vma=False,
    )
```

```python
import functools

import jax
import jax.numpy as jnp
from jax import lax
from jax.experimental import pallas as pl
from jax.experimental.pallas import tpu as pltpu
from jax.sharding import Mesh
from jax.sharding import PartitionSpec as P

HEADS = 16
KV_HEADS = 4
HEAD_DIM = 128
SHARE = HEADS // KV_HEADS

EPS = 1e-05
THETA = 10000.0
LOG2E = 1.4426950408889634
SCALE = HEAD_DIM ** (-0.5)
FAR = 1e30

AXES = ("far", "x", "core", "zh", "zl")
TEAM = ("x", "zl")

BF = jnp.bfloat16
F32 = jnp.float32


def dot(left, right, left_dim=1, right_dim=0):
    return lax.dot_general(
        left, right, (((left_dim,), (right_dim,)), ((), ())), preferred_element_type=F32
    )


def turned(values, cosine, sine):
    return values * cosine + pltpu.roll(values, HEAD_DIM // 2, axis=1) * sine


def visible(kpos, qpos, qstart):
    return (kpos <= qpos) & (kpos >= qstart)


def is_mixed(starts, base, run):
    mixed = False
    for start in starts:
        inside = (start > base) & (start < base + run)
        mixed = inside if mixed is False else (mixed | inside)
    return mixed


def run_row(meta, sizes, number, run):
    far_n, zh_n = sizes
    far, core, zh = (meta[i] for i in range(3))
    zh_r = lax.rem(number, zh_n)
    core_r = lax.rem(number // zh_n, 2)
    x_r = lax.rem(number // (2 * zh_n), 2)
    far_r = number // (4 * zh_n)
    slot = ((core_r ^ core) * far_n + (far_r ^ far)) * zh_n + (zh_r ^ zh)
    return pl.multiple_of((slot * 2 + x_r) * run, run)


def natural_slot(meta, sizes, i):
    far_n, zh_n = sizes
    far, core, zh = (meta[k] for k in range(3))
    zh_i = i % zh_n if isinstance(i, int) else lax.rem(i, zh_n)
    far_i = i // zh_n % far_n if isinstance(i, int) else lax.rem(i // zh_n, far_n)
    core_i = i // (zh_n * far_n)
    return ((core_i ^ core) * far_n + (far_i ^ far)) * zh_n + (zh_i ^ zh)


def pair_rows(meta, sizes, i, run):
    return [pl.ds(run_row(meta, sizes, 2 * i + n, run), run) for n in range(2)]


def forward_kernel(
    docs, sizes, run, count, meta, q, cosine, sine, qpos, qstart, kown, klocal, *refs
):
    low = meta[3]
    high = low + 2 * sizes[1]
    first = meta[4]
    starts = [meta[5 + d] for d in range(docs)]
    factor = SCALE * LOG2E
    tile = 2 * run
    out, q_rot, lse, kv, sems, top, total, acc = refs[count:]
    copies = load_pieces(refs[:count], kv, sems, 0)
    for copy in copies:
        copy.wait()

    heads = range(SHARE)
    for h in heads:
        lanes = slice(h * HEAD_DIM, (h + 1) * HEAD_DIM)
        q_rot[:, lanes] = turned(q[:, lanes], cosine[...], sine[...]).astype(BF)
    top[...] = jnp.full_like(top, -FAR)
    total[...] = jnp.zeros_like(total)
    acc[...] = jnp.zeros_like(acc)

    def fold(i, masked):
        base = i * tile
        rows = pair_rows(meta, sizes, i, run)
        keys = jnp.concatenate([kv[r, :HEAD_DIM] for r in rows], axis=0)
        values = jnp.concatenate([kv[r, HEAD_DIM:] for r in rows], axis=0).T
        seen = (qstart[...] <= base) & (qpos[...] >= base + tile - 1)
        if masked:
            allowed = visible(klocal[...] + base, qpos[...], qstart[...])
        for h in heads:
            lanes = slice(h * HEAD_DIM, (h + 1) * HEAD_DIM)
            raw = dot(keys, q_rot[:, lanes], 1, 1)
            before = top[h : h + 1, :]
            if masked:
                raw = jnp.where(allowed, raw, -FAR)
                peak = jnp.maximum(before, jnp.max(raw, axis=0, keepdims=True))
                level = jnp.where(peak > -0.5 * FAR, peak * factor, FAR)
            else:
                new = jnp.max(raw, axis=0, keepdims=True)
                peak = jnp.maximum(before, jnp.where(seen, new, -FAR))
                level = jnp.where(seen, peak * factor, FAR)
            weights = jnp.exp2(raw * factor - level)
            fade = jnp.exp2((before - peak) * factor)
            top[h : h + 1, :] = peak
            total[h : h + 1, :] = total[h : h + 1, :] * fade + jnp.sum(
                weights, axis=0, keepdims=True
            )
            acc[h] = acc[h] * fade + dot(values, weights.astype(BF))

    def step(i, _):
        mixed = is_mixed(starts, i * tile, tile) | (i == low // 2) | (i == high // 2)

        @pl.when(mixed)
        def _():
            fold(i, True)

        @pl.when(jnp.logical_not(mixed))
        def _():
            fold(i, False)

        return 0

    lax.fori_loop(first // 2, high // 2 + 1, step, 0)
    for h in heads:
        lanes = slice(h * HEAD_DIM, (h + 1) * HEAD_DIM)
        out[:, lanes] = (acc[h] / total[h : h + 1, :]).T.astype(BF)
    lse[...] = top[...] * factor + jnp.log2(total[...])


def load_natural(meta, sizes, source, target, sems, base):
    slots = 2 * sizes[0] * sizes[1]
    block = source.shape[0] // slots
    copies = []
    for i in range(slots):
        away = pl.ds(pl.multiple_of(natural_slot(meta, sizes, i) * block, block), block)
        copy = pltpu.make_async_copy(
            source.at[away, :], target.at[pl.ds(i * block, block), :], sems.at[base + i]
        )
        copy.start()
        copies.append(copy)
    return copies


def proj_kernel(sizes, meta, attn, w_out, proj, held, sems):
    for copy in load_natural(meta, sizes, w_out, held, sems, 0):
        copy.wait()
    for at in range(0, held.shape[0], 256):
        proj[:, at : at + 256] = dot(attn[...], held[at : at + 256, :], 1, 1).astype(BF)


def backward_kernel(
    docs, sizes, run, count, meta, q, o, g_proj, w_out, lse, cosine, sine, qpos, qstart, kown, klocal, *refs
):
    low = meta[3]
    high = low + 2 * sizes[1]
    first = meta[4]
    starts = [meta[5 + d] for d in range(docs)]
    factor = SCALE * LOG2E
    tile = 2 * run
    grad_q, grad_kv, kv, held, sems, dqt, delta, g = refs[count:]
    copies = load_pieces(refs[:count], kv, sems, 0)
    for copy in load_natural(meta, sizes, w_out, held, sems, count):
        copy.wait()
    total = dot(g_proj[...], held[...])
    for copy in copies:
        copy.wait()
    g[...] = total.astype(BF)
    dqt[...] = jnp.zeros_like(dqt)
    grad_kv[...] = jnp.zeros_like(grad_kv)

    def prepare(h, _):
        lanes = pl.ds(pl.multiple_of(h * HEAD_DIM, HEAD_DIM), HEAD_DIM)
        both = o[:, lanes].astype(F32) * g[:, lanes].astype(F32)
        delta[pl.ds(h, 1), :] = jnp.sum(both.T, axis=0, keepdims=True)
        return 0

    lax.fori_loop(0, SHARE, prepare, 0)

    def key_step(i, masked):
        base = i * tile
        rows = pair_rows(meta, sizes, i, run)
        k_tile = jnp.concatenate([kv[r, :HEAD_DIM] for r in rows], axis=0)
        v_tile = jnp.concatenate([kv[r, HEAD_DIM:] for r in rows], axis=0)
        kt = k_tile.T
        seen = (qstart[...] <= base) & (qpos[...] >= base + tile - 1)
        if masked:
            allowed = visible(klocal[...] + base, qpos[...], qstart[...])
        grad_k = jnp.zeros((tile, HEAD_DIM), F32)
        grad_v = jnp.zeros((tile, HEAD_DIM), F32)
        for h in range(SHARE):
            lanes = slice(h * HEAD_DIM, (h + 1) * HEAD_DIM)
            q_head = q[:, lanes]
            g_head = g[:, lanes]
            raw = dot(k_tile, q_head, 1, 1) * factor
            level = lse[h : h + 1, :]
            if masked:
                probs = jnp.where(allowed, jnp.exp2(raw - level), 0.0)
            else:
                probs = jnp.exp2(raw - jnp.where(seen, level, FAR))
            slopes = dot(v_tile, g_head, 1, 1)
            grads = (probs * (slopes - delta[h : h + 1, :])).astype(BF)
            grad_v = grad_v + dot(probs.astype(BF), g_head)
            grad_k = grad_k + dot(grads, q_head)
            dqt[h] = dqt[h] + dot(kt, grads)
        for n, at in enumerate(rows):
            part = slice(n * run, (n + 1) * run)
            grad_kv[at, :HEAD_DIM] = (grad_k[part] * SCALE).astype(BF)
            grad_kv[at, HEAD_DIM:] = grad_v[part].astype(BF)

    def step(i, _):
        mixed = is_mixed(starts, i * tile, tile) | (i == low // 2) | (i == high // 2)

        @pl.when(mixed)
        def _():
            key_step(i, True)

        @pl.when(jnp.logical_not(mixed))
        def _():
            key_step(i, False)

        return 0

    lax.fori_loop(first // 2, high // 2 + 1, step, 0)

    def finish(h, _):
        lanes = pl.ds(pl.multiple_of(h * HEAD_DIM, HEAD_DIM), HEAD_DIM)
        rotated = (dqt[h] * SCALE).T.astype(BF).astype(F32)
        grad_q[:, lanes] = turned(rotated, cosine[...], -sine[...]).astype(BF)
        return 0

    lax.fori_loop(0, SHARE, finish, 0)


SMEM = pl.BlockSpec(memory_space=pltpu.SMEM)
VMEM = pl.BlockSpec(memory_space=pltpu.VMEM)
ANY = pl.BlockSpec(memory_space=pl.ANY)


def attention_forward(meta, docs, sizes, q, tables, kv):
    tile = q.shape[0]
    run = tile // 2
    span = sum(a.shape[0] for a in kv)
    pairs = tile * span // 2 * SHARE
    return pl.pallas_call(
        functools.partial(forward_kernel, docs, sizes, run, len(kv)),
        out_shape=(
            jax.ShapeDtypeStruct(q.shape, BF),
            jax.ShapeDtypeStruct(q.shape, BF),
            jax.ShapeDtypeStruct((SHARE, tile), F32),
        ),
        in_specs=[SMEM] + [VMEM] * (1 + len(tables)) + [ANY] * len(kv),
        out_specs=(VMEM, VMEM, VMEM),
        scratch_shapes=[
            pltpu.VMEM((span, 2 * HEAD_DIM), BF),
            pltpu.SemaphoreType.DMA((len(kv),)),
            pltpu.VMEM((SHARE, tile), F32),
            pltpu.VMEM((SHARE, tile), F32),
            pltpu.VMEM((SHARE, HEAD_DIM, tile), F32),
        ],
        compiler_params=pltpu.CompilerParams(vmem_limit_bytes=56 << 20),
        cost_estimate=pl.CostEstimate(
            flops=pairs * HEAD_DIM * 4, bytes_accessed=4 << 20, transcendentals=pairs
        ),
        name="attention_forward",
    )(meta, q, *tables, *kv)


def attention_backward(meta, docs, sizes, q, o, g_proj, w_out, lse, tables, kv):
    tile = q.shape[0]
    run = tile // 2
    span = sum(a.shape[0] for a in kv)
    pairs = tile * span // 2 * SHARE
    return pl.pallas_call(
        functools.partial(backward_kernel, docs, sizes, run, len(kv)),
        out_shape=(
            jax.ShapeDtypeStruct(q.shape, BF),
            jax.ShapeDtypeStruct((span, 2 * HEAD_DIM), BF),
        ),
        in_specs=[SMEM, VMEM, VMEM, VMEM, ANY] + [VMEM] * (1 + len(tables)) + [ANY] * len(kv),
        out_specs=(VMEM, VMEM),
        scratch_shapes=[
            pltpu.VMEM((span, 2 * HEAD_DIM), BF),
            pltpu.VMEM(w_out.shape, BF),
            pltpu.SemaphoreType.DMA((len(kv) + 2 * sizes[0] * sizes[1],)),
            pltpu.VMEM((SHARE, HEAD_DIM, tile), F32),
            pltpu.VMEM((SHARE, tile), F32),
            pltpu.VMEM(q.shape, BF),
        ],
        compiler_params=pltpu.CompilerParams(vmem_limit_bytes=56 << 20),
        cost_estimate=pl.CostEstimate(
            flops=pairs * HEAD_DIM * 10, bytes_accessed=6 << 20, transcendentals=pairs
        ),
        name="attention_backward",
    )(meta, q, o, g_proj, w_out, lse, *tables, *kv)


def call(kernel, name, shapes, operands, specs=None, scratch=(), flops=1 << 20):
    nbytes = sum(a.size * a.dtype.itemsize for a in operands)
    return pl.pallas_call(
        kernel,
        out_shape=tuple(jax.ShapeDtypeStruct(s, d) for s, d in shapes),
        in_specs=specs or [VMEM] * len(operands),
        out_specs=(VMEM,) * len(shapes),
        scratch_shapes=list(scratch),
        compiler_params=pltpu.CompilerParams(vmem_limit_bytes=56 << 20),
        cost_estimate=pl.CostEstimate(flops=flops, bytes_accessed=nbytes, transcendentals=0),
        name=name,
    )(*operands)


def load_pieces(pieces, target, sems, base):
    copies = []
    place = 0
    for i, piece in enumerate(pieces):
        rows = piece.shape[0]
        copy = pltpu.make_async_copy(piece, target.at[pl.ds(place, rows), :], sems.at[base + i])
        copy.start()
        copies.append(copy)
        place += rows
    return copies


def pack_kernel(team, count, *refs):
    out = refs[count]
    place = 0
    for shard in refs[:count]:
        part = shard.shape[1] // team
        for t in range(team):
            out[t, :, place : place + part] = shard[:, t * part : (t + 1) * part]
        place += part


def pack(team, shards):
    width = sum(s.shape[1] for s in shards) // team
    kernel = functools.partial(pack_kernel, team, len(shards))
    return call(kernel, "pack", [((team, shards[0].shape[0], width), BF)], shards)[0]


def slots_kernel(chunk, scaled, copies, order, array, keep, own, sent):
    width = array.shape[1]
    for j in range(width // chunk):
        if chunk < width:
            block = array[:, pl.ds(pl.multiple_of(order[j] * chunk, chunk), chunk)]
        else:
            block = array[...]
        lanes = pl.ds(j * chunk, chunk)
        own[:, lanes] = block
        if scaled:
            block = (block.astype(F32) * keep[...]).astype(BF)
        for t in range(copies):
            sent[t, :, lanes] = block


def slots_and_copies(array, keep, scaled, copies):
    chunk, order = slot_order(array.shape[1], True)
    if order is None:
        array, order = to_slots(array), jnp.zeros((1,), jnp.int32)
    kernel = functools.partial(slots_kernel, chunk, scaled, copies)
    shapes = [(array.shape, BF), ((copies,) + array.shape, BF)]
    return call(kernel, "to_slots", shapes, [order, array, keep], [SMEM, VMEM, VMEM])


def natural_kernel(chunk, order, array, out):
    for j in range(array.shape[1] // chunk):
        out[:, j * chunk : (j + 1) * chunk] = array[
            :, pl.ds(pl.multiple_of(order[j] * chunk, chunk), chunk)
        ]


def to_natural(array):
    chunk, order = slot_order(array.shape[1], False)
    if order is None:
        return from_slots(array)
    kernel = functools.partial(natural_kernel, chunk)
    return call(kernel, "from_slots", [(array.shape, array.dtype)], [order, array], [SMEM, VMEM])[0]


def slot_order(width, forward):
    far_n, x_n, core_n, zh_n, _ = [lax.axis_size(a) for a in AXES]
    far, _, core, zh, _ = [lax.axis_index(a) for a in AXES]
    count = far_n * x_n * core_n * zh_n
    chunk = width // count
    if chunk % HEAD_DIM:
        return width, None
    j = lax.iota(jnp.int32, count)
    if forward:
        c, f, z, x = j // (far_n * zh_n * x_n), j // (zh_n * x_n) % far_n, j // x_n % zh_n, j % x_n
        return chunk, (((f ^ far) * x_n + x) * core_n + (c ^ core)) * zh_n + (z ^ zh)
    f, x, c, z = j // (x_n * core_n * zh_n), j // (core_n * zh_n) % x_n, j // zh_n % core_n, j % zh_n
    return chunk, (((c ^ core) * far_n + (f ^ far)) * zh_n + (z ^ zh)) * x_n + x


def project_kernel(count, ids, x, cosine, sine, *refs):
    pieces = refs[:count]
    normed, scale, q, kv, small, w, sems = refs[count:]
    copies = load_pieces(pieces, w, sems, 0)
    rows = x.shape[0]
    features = x.shape[1]
    step = 128

    def squares(i, _):
        at = pl.ds(pl.multiple_of(i * step, step), step)
        block = x[at, :].astype(F32)
        scale[at, :] = lax.rsqrt(jnp.sum(block * block, axis=1, keepdims=True) / features + EPS)
        return 0

    lax.fori_loop(0, rows // step, squares, 0)
    for copy in copies:
        copy.wait()
    width = w.shape[1] - HEAD_DIM
    turned_small = w[:, width:].astype(F32).T
    small[...] = turned_small[: small.shape[0], :]
    gain = small[ids : ids + 1, :]

    def norm(i, _):
        at = pl.ds(pl.multiple_of(i * step, step), step)
        normed[at, :] = (x[at, :].astype(F32) * scale[at, :] * gain).astype(BF)
        return 0

    lax.fori_loop(0, rows // step, norm, 0)
    for at in range(0, width - 2 * HEAD_DIM, 256):
        q[:, at : at + 256] = dot(normed[...], w[:, at : at + 256])
    both = dot(normed[...], w[:, width - 2 * HEAD_DIM : width])
    kv[:, :HEAD_DIM] = turned(both[:, :HEAD_DIM], cosine[...], sine[...]).astype(BF)
    kv[:, HEAD_DIM:] = both[:, HEAD_DIM:].astype(BF)


def project(tokens_all, cosine, sine, pieces, ids):
    rows, features = tokens_all.shape
    width = pieces[0].shape[1]
    held = -(-(ids + 2) // 8) * 8
    return call(
        functools.partial(project_kernel, len(pieces), ids),
        "project",
        [
            ((rows, features), BF),
            ((rows, 1), F32),
            ((rows, width - 3 * HEAD_DIM), F32),
            ((rows, 2 * HEAD_DIM), BF),
            ((held, features), F32),
        ],
        [tokens_all, cosine, sine, *pieces],
        [VMEM] * 3 + [ANY] * len(pieces),
        [pltpu.VMEM((features, width), BF), pltpu.SemaphoreType.DMA((len(pieces),))],
        2 * rows * features * width,
    )


def middle_kernel(parts, tokens, keep, gain, middle, sent):
    proj = total_of([parts[t] for t in range(parts.shape[0])])
    mid = tokens[...].astype(F32) + keep[...] * proj
    scale = lax.rsqrt(jnp.mean(mid * mid, axis=1, keepdims=True) + EPS)
    middle[...] = mid
    normed = (mid * scale * gain[...]).astype(BF)
    for t in range(sent.shape[0]):
        sent[t] = normed


def middle_grad_kernel(parts, middle, cotangent, keep, gain, grad_middle, sent, terms):
    grad = total_of([parts[t] for t in range(parts.shape[0])])
    mid = middle[...]
    scale = lax.rsqrt(jnp.mean(mid * mid, axis=1, keepdims=True) + EPS)
    gained = grad * gain[...]
    terms[...] = (grad * mid * scale).astype(BF)
    result = (
        cotangent[...].astype(F32)
        + scale * gained
        - mid * scale**3 * jnp.mean(gained * mid, axis=1, keepdims=True)
    )
    grad_middle[...] = result
    proj = (keep[...] * result).astype(BF)
    for t in range(sent.shape[0]):
        sent[t] = proj


def token_grad_kernel(parts, tokens, grad_middle, gain, out):
    grad = total_of([parts[t] for t in range(parts.shape[0])])
    x = tokens[...].astype(F32)
    scale = lax.rsqrt(jnp.mean(x * x, axis=1, keepdims=True) + EPS)
    gained = grad * gain[...]
    out[...] = (
        grad_middle[...]
        + scale * gained
        - x * scale**3 * jnp.mean(gained * x, axis=1, keepdims=True)
    )


def output_kernel(parts, middle, keep, out):
    ffn = total_of([parts[t] for t in range(parts.shape[0])])
    out[...] = (middle[...] + keep[...] * ffn).astype(BF)


def mlp_kernel(sizes, count, meta, x, g, gate_rows, *refs):
    pieces = refs[: 2 * count]
    hidden, grad_gate, grad_up, grad_x, ffn, w_g, w_u, w_d, sems = refs[2 * count :]
    copies = load_natural(meta, sizes, gate_rows, w_g, sems, 2 * count)
    copies += load_pieces(pieces[:count], w_u, sems, 0)
    late = load_pieces(pieces[count:], w_d, sems, count)
    for copy in copies:
        copy.wait()
    features, width = w_g.shape

    def columns(lanes, wait=()):
        gate = dot(x[...], w_g[:, lanes])
        up = dot(x[...], w_u[:, lanes])
        for copy in wait:
            copy.wait()
        grad = dot(g[...], w_d[:, lanes])
        sig = 1.0 / (1.0 + jnp.exp(-gate))
        silu = gate * sig
        hidden[:, lanes] = (silu * up).astype(BF)
        grad_gate[:, lanes] = (grad * up * sig * (1.0 + gate * (1.0 - sig))).astype(BF)
        grad_up[:, lanes] = (grad * silu).astype(BF)

    step = 256
    tail = width % step
    columns(pl.ds(width - tail, tail) if tail else pl.ds(width - step, step), late)

    def chunk(i, _):
        columns(pl.ds(pl.multiple_of(i * step, step), step))
        return 0

    lax.fori_loop(0, (width - 1) // step, chunk, 0)

    def back_rows(i, _):
        at = pl.ds(pl.multiple_of(i * step, step), step)
        total = dot(grad_gate[...], w_g[at, :], 1, 1) + dot(grad_up[...], w_u[at, :], 1, 1)
        grad_x[:, at] = total.astype(BF)
        ffn[:, at] = dot(hidden[...], w_d[at, :], 1, 1).astype(BF)
        return 0

    lax.fori_loop(0, features // step, back_rows, 0)


def mlp(meta, sizes, x, g, w_gate, w_up, w_down):
    rows, features = x.shape
    width = w_gate.shape[1]
    count = len(w_up)
    pieces = [w_gate, *w_up, *w_down]
    copies = 2 * count + 2 * sizes[0] * sizes[1]
    return call(
        functools.partial(mlp_kernel, sizes, count),
        "mlp",
        [((rows, width), BF)] * 3 + [((rows, features), BF)] * 2,
        [meta, x, g, *pieces],
        [SMEM] + [VMEM] * 2 + [ANY] * len(pieces),
        [*([pltpu.VMEM((features, width), BF)] * 3), pltpu.SemaphoreType.DMA((copies,))],
        12 * rows * features * width,
    )


def outer_kernel(meta, left, right, *refs):
    product = dot(left[...].T, right[...])
    if len(refs) == 2:
        product = product + refs[0][...].astype(F32)
    refs[-1][...] = product.astype(BF)


def outer(meta, sizes, left, right, half=None, natural=False, added=None):
    features = left.shape[1]
    if features // (2 * sizes[0] * sizes[1]) % HEAD_DIM:
        sizes_held = features if half is None else features // 2
        part = left if half is None else left[:, half * sizes_held : (half + 1) * sizes_held]
        product = dot(part, right, 0, 0)
        if natural:
            shape = (sizes[0], sizes[1], -1, right.shape[1])
            product = product.reshape(shape)
            for axis, name in enumerate(("far", "zh")):
                product = by_distance(product, axis, lax.axis_index(name))
            product = product.reshape(sizes_held, -1)
        return (product if added is None else product + added.astype(F32)).astype(BF)
    slots = 2 * sizes[0] * sizes[1]
    rows, block, width = left.shape[0], features // slots, right.shape[1]
    count, start = (slots, 0) if half is None else (slots // 2, half * slots // 2)
    held = pl.BlockSpec((block, width), lambda i, m: (i, 0))
    natural_rows = pl.BlockSpec(
        (block, width), lambda i, m: (lax.rem(natural_slot(m, sizes, i), count), 0)
    )
    return pl.pallas_call(
        outer_kernel,
        out_shape=jax.ShapeDtypeStruct((count * block, width), BF),
        grid_spec=pltpu.PrefetchScalarGridSpec(
            num_scalar_prefetch=1,
            grid=(count,),
            in_specs=[
                pl.BlockSpec((rows, block), lambda i, m: (0, start + i)),
                pl.BlockSpec((rows, width), lambda i, m: (0, 0)),
            ]
            + ([] if added is None else [natural_rows if natural else held]),
            out_specs=natural_rows if natural else held,
        ),
        compiler_params=pltpu.CompilerParams(vmem_limit_bytes=48 << 20),
        cost_estimate=pl.CostEstimate(
            flops=2 * rows * count * block * width,
            bytes_accessed=2 * count * block * (rows + width),
            transcendentals=0,
        ),
        name="outer",
    )(meta, left, right, *([] if added is None else [added]))


def qkv_grad_kernel(count, grad_q, grad_kv, x, scale, *refs):
    pieces = refs[:count]
    out, terms, w, sems = refs[count:]
    for copy in load_pieces(pieces, w, sems, 0):
        copy.wait()
    q_width = grad_q.shape[1]
    step = 256

    def rows_of(i, _):
        at = pl.ds(pl.multiple_of(i * step, step), step)
        grad = dot(grad_q[...], w[at, :q_width], 1, 1) + dot(
            grad_kv[...], w[at, q_width : q_width + 2 * HEAD_DIM], 1, 1
        )
        out[:, at] = grad.astype(BF)
        terms[:, at] = (grad * x[:, at].astype(F32) * scale[...]).astype(BF)
        return 0

    lax.fori_loop(0, w.shape[0] // step, rows_of, 0)


def qkv_grad(grad_q, grad_kv, tokens_all, scale_all, pieces):
    rows, features = tokens_all.shape
    width = pieces[0].shape[1]
    return call(
        functools.partial(qkv_grad_kernel, len(pieces)),
        "qkv_grad",
        [((rows, features), BF)] * 2,
        [grad_q, grad_kv, tokens_all, scale_all, *pieces],
        [VMEM] * 4 + [ANY] * len(pieces),
        [pltpu.VMEM((features, width), BF), pltpu.SemaphoreType.DMA((len(pieces),))],
        2 * rows * features * width,
    )


def after(value, *done):
    return lax.optimization_barrier((value, done))[0]


def together(*values):
    return lax.optimization_barrier(values)


def swap(block, axes, distance):
    size = lax.axis_size(axes)
    return lax.ppermute(block, axes, [(i, i ^ distance) for i in range(size)])


def by_distance(array, axis, index):
    size = array.shape[axis]
    bit = 1
    while bit < size:
        shape = array.shape[:axis] + (size // (2 * bit), 2, bit) + array.shape[axis + 1 :]
        pairs = array.reshape(shape)
        flipped = jnp.flip(pairs, axis + 1)
        array = jnp.where((index & bit) != 0, flipped, pairs).reshape(array.shape)
        bit *= 2
    return array


def halves(array):
    half = array.shape[1] // 2
    return array[:, :half], array[:, half:]


def to_team(pieces):
    return lax.all_to_all(pieces, TEAM, split_axis=0, concat_axis=0, tiled=True)


def sum_team(partial):
    team = lax.axis_size(TEAM)
    return to_team(partial.reshape(team, partial.shape[0] // team, partial.shape[1]))


def total_of(parts):
    total = parts[0].astype(F32)
    for i in range(1, len(parts)):
        total = total + parts[i].astype(F32)
    return total


def plane_direct(block):
    size = lax.axis_size("far") * lax.axis_size("zh")
    return [block] + [swap(block, ("far", "zh"), d) for d in range(1, size)]


def plane_first(block):
    near = [swap(block, "zh", d) for d in range(1, lax.axis_size("zh"))]
    far = [[swap(block, "far", d)] for d in range(1, lax.axis_size("far"))]
    return block, near, far


def plane_second(first, *done):
    block, near, far = first
    if done:
        near = after(near, *done)
    far = [f + [swap(b, "far", d + 1) for b in near] for d, f in enumerate(far)]
    return sum(far, [block] + near)


def both_cores(plane):
    if len(plane) > 4:
        plane = [jnp.concatenate(plane, axis=0)]
    return list(plane) + [swap(b, "core", 1) for b in plane]


def sum_axis(part, axis, *done):
    size = lax.axis_size(axis)
    rows = part.shape[0] // size
    got = [swap(part[d * rows : (d + 1) * rows], axis, d) for d in range(1, size)]
    if done:
        got = after(got, *done)
    return total_of([part[:rows]] + got).astype(BF)


SLOT = ("core", "far", "zh")


def spread(block):
    return lax.all_gather(block, SLOT, axis=0, tiled=True)


def gather_back(partial):
    return lax.psum_scatter(partial, ("far", "zh"), scatter_dimension=0, tiled=True)


def to_owner(part):
    team = lax.axis_size(TEAM)
    return to_team(part.reshape(team, part.shape[0] // team, part.shape[1]))


def wide(pieces):
    return pieces.transpose(1, 0, 2).reshape(pieces.shape[1], -1).astype(F32)


def turn(values, cosine, sine):
    half = HEAD_DIM // 2
    other = jnp.concatenate([values[:, half:], values[:, :half]], axis=1)
    return values * cosine + other * sine


def to_slots(array):
    sizes = [lax.axis_size(a) for a in AXES]
    rows, width = array.shape
    grid = array.reshape(rows, *sizes[:4], width // (sizes[0] * sizes[1] * sizes[2] * sizes[3]))
    for axis in (0, 2, 3):
        grid = by_distance(grid, axis + 1, lax.axis_index(AXES[axis]))
    return grid.transpose(0, 3, 1, 4, 2, 5).reshape(rows, width)


def from_slots(array):
    far, x, core, zh, zl = [lax.axis_size(a) for a in AXES]
    rows, width = array.shape
    grid = array.reshape(rows, core, far, zh, x, width // (core * far * zh * x))
    grid = grid.transpose(0, 2, 4, 1, 3, 5)
    for axis in (0, 2, 3):
        grid = by_distance(grid, axis + 1, lax.axis_index(AXES[axis]))
    return grid.reshape(rows, width)


def per_device(
    tokens,
    segment_ids,
    layer_skip,
    attn_gain,
    w_query,
    w_key,
    w_value,
    w_output,
    mlp_gain,
    w_gate,
    w_up,
    w_down,
    cotangent,
):
    far_n, x_n, core_n, zh_n, zl_n = [lax.axis_size(a) for a in AXES]
    far, x, core, zh, zl = [lax.axis_index(a) for a in AXES]
    team = x_n * zl_n
    rows = tokens.shape[0]
    tile = team * rows
    run = zl_n * rows
    docs = layer_skip.shape[0]
    part = HEADS * HEAD_DIM // team
    ff = w_gate.shape[1] // team
    width = attn_gain.shape[0]
    features = tokens.shape[1]

    ids = rows // width
    doc_index = lax.iota(jnp.int32, docs)
    skipped = jnp.sum(
        jnp.where(segment_ids[:, None] == doc_index[None, :], layer_skip[None, :], 0), axis=1
    )
    keep = (1 - skipped).astype(F32)[:, None]
    small = jnp.concatenate(
        [segment_ids.astype(BF).reshape(width, ids), attn_gain[:, None], mlp_gain[:, None]], axis=1
    )
    small = jnp.pad(small, ((0, 0), (0, HEAD_DIM - ids - 2)))
    small = jnp.concatenate([small] * team, axis=1)
    first_rows = to_team(pack(team, [w_query, w_key, w_value, small, w_output.T, w_gate]))
    first_rows = first_rows.reshape(-1, first_rows.shape[2])
    qkv_width = part + 3 * HEAD_DIM
    qkv_plane = plane_first(first_rows[:, :qkv_width])
    out_rows = first_rows[:, qkv_width : qkv_width + part]
    gate_rows = first_rows[:, qkv_width + part :]

    last_rows = pack(team, [w_up, w_down.T])
    tokens_own, tokens_sent = slots_and_copies(tokens, keep, False, team)
    cot_own, cot_sent = slots_and_copies(cotangent, keep, True, team)
    tokens_all = to_team(after(tokens_sent, first_rows)).reshape(tile, features)

    local = lax.iota(jnp.int32, tile)
    place = (local // run) * (core_n * zh_n * run) + local % run
    position = ((far * x_n * core_n + core) * zh_n + zh) * run + place
    rates = jnp.power(THETA, -lax.iota(jnp.int32, HEAD_DIM // 2).astype(F32) / (HEAD_DIM // 2))
    angles = position.astype(F32)[:, None] * rates[None, :]
    cosine = jnp.cos(angles)
    sine = jnp.sin(angles)
    cosine = jnp.concatenate([cosine, cosine], axis=1)
    sine = jnp.concatenate([-sine, sine], axis=1)

    qkv_plane, last_rows, cot_sent, tokens_all = together(
        qkv_plane, last_rows, cot_sent, tokens_all
    )
    w_out = spread(after(out_rows, qkv_plane))
    w_qkv = both_cores(plane_second(qkv_plane))
    tokens_all, w_qkv, cosine, sine = together(tokens_all, w_qkv, cosine, sine)
    last_rows = to_team(after(last_rows, tokens_all)).reshape(-1, last_rows.shape[2])

    normed_one, scale_all, q, kv, small_all = project(tokens_all, cosine, sine, w_qkv, ids)
    kv_plane = plane_first(kv)
    w_g = spread(after(gate_rows, kv))
    gain_one = small_all[ids : ids + 1]
    gain_two = small_all[ids + 1 : ids + 2]
    doc_starts = jnp.sum(
        (small_all[None, :ids] < doc_index.astype(F32)[:, None, None]).astype(F32), axis=(1, 2)
    ).astype(jnp.int32)
    query_seg = jnp.sum((position[:, None] >= doc_starts[None, 1:]).astype(jnp.int32), axis=1)
    query_start = jnp.sum(
        jnp.where(query_seg[:, None] == doc_index[None, :], doc_starts[None, :], 0), axis=1
    )
    low = (far * x_n * core_n + core) * zh_n + zh
    first_start = jnp.max(jnp.where(doc_starts <= low * run, doc_starts, 0))
    meta = jnp.concatenate([jnp.stack([far, core, zh, low, first_start // run]), doc_starts])
    sizes = (far_n, zh_n)
    tables = (
        cosine,
        sine,
        position[None, :],
        query_start[None, :],
        position[:, None],
        lax.iota(jnp.int32, tile)[:, None],
    )
    up_rows, down_rows = last_rows[:, :ff], last_rows[:, ff:]
    kv_plane, meta, tables = together(kv_plane, meta, tables)
    kv_plane = plane_second(kv_plane)
    kv_plane, w_out, up_rows, down_rows = together(kv_plane, w_out, up_rows, down_rows)
    grad_ffn = to_team(after(cot_sent, up_rows))
    kv = both_cores(kv_plane)
    up_plane = plane_first(up_rows)
    attn, query, log_total = attention_forward(meta, docs, sizes, q, tables, kv)
    attn, grad_ffn, up_plane, w_g = together(attn, grad_ffn, up_plane, w_g)
    grad_ffn = grad_ffn.reshape(tile, features)

    proj = call(
        functools.partial(proj_kernel, sizes),
        "proj",
        [((tile, features), BF)],
        [meta, attn, w_out],
        [SMEM, VMEM, ANY],
        [pltpu.VMEM(w_out.shape, BF), pltpu.SemaphoreType.DMA((2 * far_n * zh_n,))],
    )[0]
    down_plane = plane_first(after(down_rows, attn))
    proj = sum_team(proj)
    up_plane = plane_second(up_plane)
    proj, up_plane, down_plane = together(proj, up_plane, down_plane)
    middle, normed_sent = call(
        middle_kernel,
        "middle",
        [((rows, features), F32), ((team, rows, features), BF)],
        [proj, tokens_own, keep, gain_two],
    )
    normed_two = to_team(normed_sent)
    w_u = both_cores(up_plane)
    w_d = both_cores(plane_second(down_plane))
    normed_two, w_u, w_d = together(normed_two, w_u, w_d)
    normed_two = normed_two.reshape(tile, features)

    hidden, grad_gate_act, grad_up_act, grad_two, ffn = mlp(
        meta, sizes, normed_two, grad_ffn, w_g, w_u, w_d
    )
    grad_two_parts = sum_team(grad_two)
    other_down = swap(outer(meta, sizes, grad_ffn, hidden, 1, True), "core", 1)
    other_gate = swap(outer(meta, sizes, normed_two, grad_gate_act, 1), "core", 1)
    other_up = swap(outer(meta, sizes, normed_two, grad_up_act, 1), "core", 1)
    grad_down = gather_back(outer(meta, sizes, grad_ffn, hidden, 0, True, other_down))
    gate_core = outer(meta, sizes, normed_two, grad_gate_act, 0, False, other_gate)
    up_core = outer(meta, sizes, normed_two, grad_up_act, 0, False, other_up)
    grad_two_parts, gate_core = together(grad_two_parts, gate_core)
    grad_middle, grad_proj_sent, terms_two = call(
        middle_grad_kernel,
        "middle_grad",
        [((rows, features), F32), ((team, rows, features), BF), ((rows, features), BF)],
        [grad_two_parts, middle, cot_own, keep, gain_two],
    )
    grad_proj = to_team(grad_proj_sent)
    gate_far = sum_axis(gate_core, "far", grad_proj_sent)
    grad_proj, up_core, gate_far = together(grad_proj, up_core, gate_far)
    grad_proj = grad_proj.reshape(tile, features)
    ffn = sum_team(after(ffn, grad_proj))
    grad_query, grad_kv = attention_backward(
        meta, docs, sizes, query, attn, grad_proj, w_out, log_total, tables, kv
    )
    gate_zh = sum_axis(gate_far, "zh", grad_kv)
    up_far = sum_axis(up_core, "far", grad_kv)
    grad_query, grad_kv, ffn, gate_zh, up_far, grad_down = together(
        grad_query, grad_kv, ffn, gate_zh, up_far, grad_down
    )
    half = grad_kv.shape[0] // 2
    other_kv = swap(grad_kv[half:], "core", 1)
    grad_query = after(grad_query, other_kv)
    attn_late = after(attn, other_kv)
    grad_kv = grad_kv[:half].astype(F32) + other_kv.astype(F32)
    grad_kv_parts = [grad_kv[:tile]] + [
        swap(grad_kv[d * tile : (d + 1) * tile].astype(BF), ("far", "zh"), d)
        for d in range(1, far_n * zh_n)
    ]
    output = to_natural(
        call(output_kernel, "output", [((rows, features), BF)], [ffn, middle, keep])[0]
    )
    other_q = jnp.concatenate(
        [
            outer(meta, sizes, normed_one, grad_query, half=1),
            outer(meta, sizes, grad_proj, attn_late, half=1),
        ],
        axis=1,
    )
    other_q = swap(other_q, "core", 1)
    own_q = jnp.concatenate(
        [
            outer(meta, sizes, normed_one, grad_query, half=0),
            outer(meta, sizes, grad_proj, attn_late, half=0),
        ],
        axis=1,
    )
    q_core = (own_q.astype(F32) + other_q.astype(F32)).astype(BF)
    grad_kv_parts, q_core = together(grad_kv_parts, q_core)
    q_far = sum_axis(q_core, "far")
    up_zh = sum_axis(after(up_far, grad_kv_parts), "zh")
    grad_kv_sum = total_of(grad_kv_parts)
    grad_key = turn(grad_kv_sum[:, :HEAD_DIM].astype(BF).astype(F32), cosine, -sine).astype(BF)
    grad_kv_tok = jnp.concatenate([grad_key, grad_kv_sum[:, HEAD_DIM:].astype(BF)], axis=1)
    grad_one, terms_one = qkv_grad(grad_query, grad_kv_tok, tokens_all, scale_all, w_qkv)
    grad_one = sum_team(grad_one)

    lanes = lax.broadcasted_iota(jnp.int32, (tile + rows, HEAD_DIM), 1)
    which = lax.broadcasted_iota(jnp.int32, (tile + rows, HEAD_DIM), 0) // tile
    pick = (lanes == which).astype(BF)
    terms = jnp.concatenate([terms_one, terms_two], axis=0)
    other_small, own_small = [
        jnp.concatenate(
            [
                outer(meta, sizes, normed_one, grad_kv_tok, half=i),
                outer(meta, sizes, terms, pick, half=i),
            ],
            axis=1,
        )
        for i in (1, 0)
    ]
    other_small = swap(other_small, "core", 1)
    small_core = (own_small.astype(F32) + other_small.astype(F32)).astype(BF)
    grad_one, small_core, q_far, up_zh = together(grad_one, small_core, q_far, up_zh)
    q_zh = sum_axis(q_far, "zh")
    rows_held = small_core.shape[0] // (far_n * zh_n)
    small_sum = total_of(
        [small_core[:rows_held]]
        + [
            swap(small_core[d * rows_held : (d + 1) * rows_held], ("far", "zh"), d)
            for d in range(1, far_n * zh_n)
        ]
    ).astype(BF)
    merged = to_owner(jnp.concatenate([grad_down, gate_zh, up_zh], axis=1))
    grad_down, grad_gate, grad_up = (
        merged[:, :, :ff], merged[:, :, ff : 2 * ff], merged[:, :, 2 * ff :]
    )
    grad_tokens = to_natural(
        call(
            token_grad_kernel,
            "token_grad",
            [((rows, features), F32)],
            [grad_one, tokens_own, grad_middle, gain_one],
        )[0]
    )
    finished = [wide(grad_gate), wide(grad_up), wide(grad_down).T]
    grad_w = jnp.concatenate([q_zh, small_sum], axis=1)
    grad_w, finished, output, grad_tokens = together(grad_w, finished, output, grad_tokens)
    grad_w = to_owner(grad_w)
    grad_out = grad_w[:, :, part : 2 * part]
    grad_w = jnp.concatenate([grad_w[:, :, :part], grad_w[:, :, 2 * part :]], axis=2)
    gains = total_of(grad_w[:, :, part + 2 * HEAD_DIM :])
    return (
        output,
        grad_tokens,
        gains[:, 0],
        wide(grad_w[:, :, :part]),
        wide(grad_w[:, :, part : part + HEAD_DIM]),
        wide(grad_w[:, :, part + HEAD_DIM : part + 2 * HEAD_DIM]),
        wide(grad_out).T,
        gains[:, 1],
        *finished,
    )


def solution(mesh):
    blk, uly = mesh.shape["blk"], mesh.shape["uly"]
    grid = Mesh(mesh.devices.reshape(blk // 4, 2, 2, uly // 2, 2), AXES)
    rows = P(AXES, None)
    cols = P(None, AXES)
    flat = P(AXES)
    return jax.shard_map(
        per_device,
        mesh=grid,
        in_specs=(
            rows, flat, P(), flat, rows, rows, rows, cols, flat, rows, rows, cols, rows,
        ),
        out_specs=(rows, rows, flat, rows, rows, rows, cols, flat, rows, rows, cols),
        check_vma=False,
    )
```

```python
import functools

import jax
import jax.numpy as jnp
from jax import lax
from jax.experimental import pallas as pl
from jax.experimental.pallas import tpu as pltpu
from jax.sharding import Mesh
from jax.sharding import PartitionSpec as P

HEADS = 16
KV_HEADS = 4
HEAD_DIM = 128
SHARE = HEADS // KV_HEADS

EPS = 1e-05
THETA = 10000.0
LOG2E = 1.4426950408889634
SCALE = HEAD_DIM ** (-0.5)
FAR = 1e30

AXES = ("far", "x", "core", "zh", "zl")
TEAM = ("x", "zl")

BF = jnp.bfloat16
F32 = jnp.float32


def dot(left, right, left_dim=1, right_dim=0):
    return lax.dot_general(
        left, right, (((left_dim,), (right_dim,)), ((), ())), preferred_element_type=F32
    )


def turned(values, cosine, sine):
    return values * cosine + pltpu.roll(values, HEAD_DIM // 2, axis=1) * sine


def visible(kpos, qpos, qstart):
    return (kpos <= qpos) & (kpos >= qstart)


def is_mixed(starts, base, run):
    mixed = False
    for start in starts:
        inside = (start > base) & (start < base + run)
        mixed = inside if mixed is False else (mixed | inside)
    return mixed


def run_row(meta, sizes, number, run):
    far_n, zh_n = sizes
    far, core, zh = (meta[i] for i in range(3))
    zh_r = lax.rem(number, zh_n)
    core_r = lax.rem(number // zh_n, 2)
    x_r = lax.rem(number // (2 * zh_n), 2)
    far_r = number // (4 * zh_n)
    slot = ((core_r ^ core) * far_n + (far_r ^ far)) * zh_n + (zh_r ^ zh)
    return pl.multiple_of((slot * 2 + x_r) * run, run)


def natural_slot(meta, sizes, i):
    far_n, zh_n = sizes
    far, core, zh = (meta[k] for k in range(3))
    zh_i = i % zh_n if isinstance(i, int) else lax.rem(i, zh_n)
    far_i = i // zh_n % far_n if isinstance(i, int) else lax.rem(i // zh_n, far_n)
    core_i = i // (zh_n * far_n)
    return ((core_i ^ core) * far_n + (far_i ^ far)) * zh_n + (zh_i ^ zh)


def pair_rows(meta, sizes, i, run):
    return [pl.ds(run_row(meta, sizes, 2 * i + n, run), run) for n in range(2)]


def forward_kernel(
    docs, sizes, run, count, meta, q, cosine, sine, qpos, qstart, kown, klocal, *refs
):
    low = meta[3]
    high = low + 2 * sizes[1]
    first = meta[4]
    starts = [meta[5 + d] for d in range(docs)]
    factor = SCALE * LOG2E
    tile = 2 * run
    out, q_rot, lse, kv, sems, top, total, acc = refs[count:]
    copies = load_pieces(refs[:count], kv, sems, 0)
    for copy in copies:
        copy.wait()

    heads = range(SHARE)
    for h in heads:
        lanes = slice(h * HEAD_DIM, (h + 1) * HEAD_DIM)
        q_rot[:, lanes] = turned(q[:, lanes], cosine[...], sine[...]).astype(BF)
    top[...] = jnp.full_like(top, -FAR)
    total[...] = jnp.zeros_like(total)
    acc[...] = jnp.zeros_like(acc)

    def fold(i, masked):
        base = i * tile
        rows = pair_rows(meta, sizes, i, run)
        keys = jnp.concatenate([kv[r, :HEAD_DIM] for r in rows], axis=0)
        values = jnp.concatenate([kv[r, HEAD_DIM:] for r in rows], axis=0).T
        seen = (qstart[...] <= base) & (qpos[...] >= base + tile - 1)
        if masked:
            allowed = visible(klocal[...] + base, qpos[...], qstart[...])
        for h in heads:
            lanes = slice(h * HEAD_DIM, (h + 1) * HEAD_DIM)
            raw = dot(keys, q_rot[:, lanes], 1, 1)
            before = top[h : h + 1, :]
            if masked:
                raw = jnp.where(allowed, raw, -FAR)
                peak = jnp.maximum(before, jnp.max(raw, axis=0, keepdims=True))
                level = jnp.where(peak > -0.5 * FAR, peak * factor, FAR)
            else:
                new = jnp.max(raw, axis=0, keepdims=True)
                peak = jnp.maximum(before, jnp.where(seen, new, -FAR))
                level = jnp.where(seen, peak * factor, FAR)
            weights = jnp.exp2(raw * factor - level)
            fade = jnp.exp2((before - peak) * factor)
            top[h : h + 1, :] = peak
            total[h : h + 1, :] = total[h : h + 1, :] * fade + jnp.sum(
                weights, axis=0, keepdims=True
            )
            acc[h] = acc[h] * fade + dot(values, weights.astype(BF))

    def step(i, _):
        mixed = is_mixed(starts, i * tile, tile) | (i == low // 2) | (i == high // 2)

        @pl.when(mixed)
        def _():
            fold(i, True)

        @pl.when(jnp.logical_not(mixed))
        def _():
            fold(i, False)

        return 0

    lax.fori_loop(first // 2, high // 2 + 1, step, 0)
    for h in heads:
        lanes = slice(h * HEAD_DIM, (h + 1) * HEAD_DIM)
        out[:, lanes] = (acc[h] / total[h : h + 1, :]).T.astype(BF)
    lse[...] = top[...] * factor + jnp.log2(total[...])


def load_natural(meta, sizes, source, target, sems, base):
    slots = 2 * sizes[0] * sizes[1]
    block = source.shape[0] // slots
    copies = []
    for i in range(slots):
        away = pl.ds(pl.multiple_of(natural_slot(meta, sizes, i) * block, block), block)
        copy = pltpu.make_async_copy(
            source.at[away, :], target.at[pl.ds(i * block, block), :], sems.at[base + i]
        )
        copy.start()
        copies.append(copy)
    return copies


def proj_kernel(sizes, meta, attn, w_out, proj, held, sems):
    for copy in load_natural(meta, sizes, w_out, held, sems, 0):
        copy.wait()
    for at in range(0, held.shape[0], 256):
        proj[:, at : at + 256] = dot(attn[...], held[at : at + 256, :], 1, 1).astype(BF)


def backward_kernel(
    docs, sizes, run, count, meta, q, o, g_proj, w_out, lse, cosine, sine, qpos, qstart, kown, klocal, *refs
):
    low = meta[3]
    high = low + 2 * sizes[1]
    first = meta[4]
    starts = [meta[5 + d] for d in range(docs)]
    factor = SCALE * LOG2E
    tile = 2 * run
    grad_q, grad_kv, kv, held, sems, dqt, delta, g = refs[count:]
    copies = load_pieces(refs[:count], kv, sems, 0)
    for copy in load_natural(meta, sizes, w_out, held, sems, count):
        copy.wait()
    total = dot(g_proj[...], held[...])
    for copy in copies:
        copy.wait()
    g[...] = total.astype(BF)
    dqt[...] = jnp.zeros_like(dqt)
    grad_kv[...] = jnp.zeros_like(grad_kv)

    def prepare(h, _):
        lanes = pl.ds(pl.multiple_of(h * HEAD_DIM, HEAD_DIM), HEAD_DIM)
        both = o[:, lanes].astype(F32) * g[:, lanes].astype(F32)
        delta[pl.ds(h, 1), :] = jnp.sum(both.T, axis=0, keepdims=True)
        return 0

    lax.fori_loop(0, SHARE, prepare, 0)

    def key_step(i, masked):
        base = i * tile
        rows = pair_rows(meta, sizes, i, run)
        k_tile = jnp.concatenate([kv[r, :HEAD_DIM] for r in rows], axis=0)
        v_tile = jnp.concatenate([kv[r, HEAD_DIM:] for r in rows], axis=0)
        kt = k_tile.T
        seen = (qstart[...] <= base) & (qpos[...] >= base + tile - 1)
        if masked:
            allowed = visible(klocal[...] + base, qpos[...], qstart[...])
        grad_k = jnp.zeros((tile, HEAD_DIM), F32)
        grad_v = jnp.zeros((tile, HEAD_DIM), F32)
        for h in range(SHARE):
            lanes = slice(h * HEAD_DIM, (h + 1) * HEAD_DIM)
            q_head = q[:, lanes]
            g_head = g[:, lanes]
            raw = dot(k_tile, q_head, 1, 1) * factor
            level = lse[h : h + 1, :]
            if masked:
                probs = jnp.where(allowed, jnp.exp2(raw - level), 0.0)
            else:
                probs = jnp.exp2(raw - jnp.where(seen, level, FAR))
            slopes = dot(v_tile, g_head, 1, 1)
            grads = (probs * (slopes - delta[h : h + 1, :])).astype(BF)
            grad_v = grad_v + dot(probs.astype(BF), g_head)
            grad_k = grad_k + dot(grads, q_head)
            dqt[h] = dqt[h] + dot(kt, grads)
        for n, at in enumerate(rows):
            part = slice(n * run, (n + 1) * run)
            grad_kv[at, :HEAD_DIM] = (grad_k[part] * SCALE).astype(BF)
            grad_kv[at, HEAD_DIM:] = grad_v[part].astype(BF)

    def step(i, _):
        mixed = is_mixed(starts, i * tile, tile) | (i == low // 2) | (i == high // 2)

        @pl.when(mixed)
        def _():
            key_step(i, True)

        @pl.when(jnp.logical_not(mixed))
        def _():
            key_step(i, False)

        return 0

    lax.fori_loop(first // 2, high // 2 + 1, step, 0)

    def finish(h, _):
        lanes = pl.ds(pl.multiple_of(h * HEAD_DIM, HEAD_DIM), HEAD_DIM)
        rotated = (dqt[h] * SCALE).T.astype(BF).astype(F32)
        grad_q[:, lanes] = turned(rotated, cosine[...], -sine[...]).astype(BF)
        return 0

    lax.fori_loop(0, SHARE, finish, 0)


SMEM = pl.BlockSpec(memory_space=pltpu.SMEM)
VMEM = pl.BlockSpec(memory_space=pltpu.VMEM)
ANY = pl.BlockSpec(memory_space=pl.ANY)


def attention_forward(meta, docs, sizes, q, tables, kv):
    tile = q.shape[0]
    run = tile // 2
    span = sum(a.shape[0] for a in kv)
    pairs = tile * span // 2 * SHARE
    return pl.pallas_call(
        functools.partial(forward_kernel, docs, sizes, run, len(kv)),
        out_shape=(
            jax.ShapeDtypeStruct(q.shape, BF),
            jax.ShapeDtypeStruct(q.shape, BF),
            jax.ShapeDtypeStruct((SHARE, tile), F32),
        ),
        in_specs=[SMEM] + [VMEM] * (1 + len(tables)) + [ANY] * len(kv),
        out_specs=(VMEM, VMEM, VMEM),
        scratch_shapes=[
            pltpu.VMEM((span, 2 * HEAD_DIM), BF),
            pltpu.SemaphoreType.DMA((len(kv),)),
            pltpu.VMEM((SHARE, tile), F32),
            pltpu.VMEM((SHARE, tile), F32),
            pltpu.VMEM((SHARE, HEAD_DIM, tile), F32),
        ],
        compiler_params=pltpu.CompilerParams(vmem_limit_bytes=56 << 20),
        cost_estimate=pl.CostEstimate(
            flops=pairs * HEAD_DIM * 4, bytes_accessed=4 << 20, transcendentals=pairs
        ),
        name="attention_forward",
    )(meta, q, *tables, *kv)


def attention_backward(meta, docs, sizes, q, o, g_proj, w_out, lse, tables, kv):
    tile = q.shape[0]
    run = tile // 2
    span = sum(a.shape[0] for a in kv)
    pairs = tile * span // 2 * SHARE
    return pl.pallas_call(
        functools.partial(backward_kernel, docs, sizes, run, len(kv)),
        out_shape=(
            jax.ShapeDtypeStruct(q.shape, BF),
            jax.ShapeDtypeStruct((span, 2 * HEAD_DIM), BF),
        ),
        in_specs=[SMEM, VMEM, VMEM, VMEM, ANY] + [VMEM] * (1 + len(tables)) + [ANY] * len(kv),
        out_specs=(VMEM, VMEM),
        scratch_shapes=[
            pltpu.VMEM((span, 2 * HEAD_DIM), BF),
            pltpu.VMEM(w_out.shape, BF),
            pltpu.SemaphoreType.DMA((len(kv) + 2 * sizes[0] * sizes[1],)),
            pltpu.VMEM((SHARE, HEAD_DIM, tile), F32),
            pltpu.VMEM((SHARE, tile), F32),
            pltpu.VMEM(q.shape, BF),
        ],
        compiler_params=pltpu.CompilerParams(vmem_limit_bytes=56 << 20),
        cost_estimate=pl.CostEstimate(
            flops=pairs * HEAD_DIM * 10, bytes_accessed=6 << 20, transcendentals=pairs
        ),
        name="attention_backward",
    )(meta, q, o, g_proj, w_out, lse, *tables, *kv)


def call(kernel, name, shapes, operands, specs=None, scratch=(), flops=1 << 20):
    nbytes = sum(a.size * a.dtype.itemsize for a in operands)
    return pl.pallas_call(
        kernel,
        out_shape=tuple(jax.ShapeDtypeStruct(s, d) for s, d in shapes),
        in_specs=specs or [VMEM] * len(operands),
        out_specs=(VMEM,) * len(shapes),
        scratch_shapes=list(scratch),
        compiler_params=pltpu.CompilerParams(vmem_limit_bytes=56 << 20),
        cost_estimate=pl.CostEstimate(flops=flops, bytes_accessed=nbytes, transcendentals=0),
        name=name,
    )(*operands)


def load_pieces(pieces, target, sems, base):
    copies = []
    place = 0
    for i, piece in enumerate(pieces):
        rows = piece.shape[0]
        copy = pltpu.make_async_copy(piece, target.at[pl.ds(place, rows), :], sems.at[base + i])
        copy.start()
        copies.append(copy)
        place += rows
    return copies


def pack_kernel(team, count, *refs):
    out = refs[count]
    place = 0
    for shard in refs[:count]:
        part = shard.shape[1] // team
        for t in range(team):
            out[t, :, place : place + part] = shard[:, t * part : (t + 1) * part]
        place += part


def pack(team, shards):
    width = sum(s.shape[1] for s in shards) // team
    kernel = functools.partial(pack_kernel, team, len(shards))
    return call(kernel, "pack", [((team, shards[0].shape[0], width), BF)], shards)[0]


def slots_kernel(chunk, scaled, copies, order, array, keep, own, sent):
    width = array.shape[1]
    for j in range(width // chunk):
        if chunk < width:
            block = array[:, pl.ds(pl.multiple_of(order[j] * chunk, chunk), chunk)]
        else:
            block = array[...]
        lanes = pl.ds(j * chunk, chunk)
        own[:, lanes] = block
        if scaled:
            block = (block.astype(F32) * keep[...]).astype(BF)
        for t in range(copies):
            sent[t, :, lanes] = block


def slots_and_copies(array, keep, scaled, copies):
    chunk, order = slot_order(array.shape[1], True)
    if order is None:
        array, order = to_slots(array), jnp.zeros((1,), jnp.int32)
    kernel = functools.partial(slots_kernel, chunk, scaled, copies)
    shapes = [(array.shape, BF), ((copies,) + array.shape, BF)]
    return call(kernel, "to_slots", shapes, [order, array, keep], [SMEM, VMEM, VMEM])


def natural_kernel(chunk, order, array, out):
    for j in range(array.shape[1] // chunk):
        out[:, j * chunk : (j + 1) * chunk] = array[
            :, pl.ds(pl.multiple_of(order[j] * chunk, chunk), chunk)
        ]


def to_natural(array):
    chunk, order = slot_order(array.shape[1], False)
    if order is None:
        return from_slots(array)
    kernel = functools.partial(natural_kernel, chunk)
    return call(kernel, "from_slots", [(array.shape, array.dtype)], [order, array], [SMEM, VMEM])[0]


def slot_order(width, forward):
    far_n, x_n, core_n, zh_n, _ = [lax.axis_size(a) for a in AXES]
    far, _, core, zh, _ = [lax.axis_index(a) for a in AXES]
    count = far_n * x_n * core_n * zh_n
    chunk = width // count
    if chunk % HEAD_DIM:
        return width, None
    j = lax.iota(jnp.int32, count)
    if forward:
        c, f, z, x = j // (far_n * zh_n * x_n), j // (zh_n * x_n) % far_n, j // x_n % zh_n, j % x_n
        return chunk, (((f ^ far) * x_n + x) * core_n + (c ^ core)) * zh_n + (z ^ zh)
    f, x, c, z = j // (x_n * core_n * zh_n), j // (core_n * zh_n) % x_n, j // zh_n % core_n, j % zh_n
    return chunk, (((c ^ core) * far_n + (f ^ far)) * zh_n + (z ^ zh)) * x_n + x


def project_kernel(count, ids, x, cosine, sine, *refs):
    pieces = refs[:count]
    normed, scale, q, kv, small, w, sems = refs[count:]
    copies = load_pieces(pieces, w, sems, 0)
    rows = x.shape[0]
    features = x.shape[1]
    step = 128

    def squares(i, _):
        at = pl.ds(pl.multiple_of(i * step, step), step)
        block = x[at, :].astype(F32)
        scale[at, :] = lax.rsqrt(jnp.sum(block * block, axis=1, keepdims=True) / features + EPS)
        return 0

    lax.fori_loop(0, rows // step, squares, 0)
    for copy in copies:
        copy.wait()
    width = w.shape[1] - HEAD_DIM
    turned_small = w[:, width:].astype(F32).T
    small[...] = turned_small[: small.shape[0], :]
    gain = small[ids : ids + 1, :]

    def norm(i, _):
        at = pl.ds(pl.multiple_of(i * step, step), step)
        normed[at, :] = (x[at, :].astype(F32) * scale[at, :] * gain).astype(BF)
        return 0

    lax.fori_loop(0, rows // step, norm, 0)
    for at in range(0, width - 2 * HEAD_DIM, 256):
        q[:, at : at + 256] = dot(normed[...], w[:, at : at + 256])
    both = dot(normed[...], w[:, width - 2 * HEAD_DIM : width])
    kv[:, :HEAD_DIM] = turned(both[:, :HEAD_DIM], cosine[...], sine[...]).astype(BF)
    kv[:, HEAD_DIM:] = both[:, HEAD_DIM:].astype(BF)


def project(tokens_all, cosine, sine, pieces, ids):
    rows, features = tokens_all.shape
    width = pieces[0].shape[1]
    held = -(-(ids + 2) // 8) * 8
    return call(
        functools.partial(project_kernel, len(pieces), ids),
        "project",
        [
            ((rows, features), BF),
            ((rows, 1), F32),
            ((rows, width - 3 * HEAD_DIM), F32),
            ((rows, 2 * HEAD_DIM), BF),
            ((held, features), F32),
        ],
        [tokens_all, cosine, sine, *pieces],
        [VMEM] * 3 + [ANY] * len(pieces),
        [pltpu.VMEM((features, width), BF), pltpu.SemaphoreType.DMA((len(pieces),))],
        2 * rows * features * width,
    )


def middle_kernel(parts, tokens, keep, gain, middle, sent):
    proj = total_of([parts[t] for t in range(parts.shape[0])])
    mid = tokens[...].astype(F32) + keep[...] * proj
    scale = lax.rsqrt(jnp.mean(mid * mid, axis=1, keepdims=True) + EPS)
    middle[...] = mid
    normed = (mid * scale * gain[...]).astype(BF)
    for t in range(sent.shape[0]):
        sent[t] = normed


def middle_grad_kernel(parts, middle, cotangent, keep, gain, grad_middle, sent, terms):
    grad = total_of([parts[t] for t in range(parts.shape[0])])
    mid = middle[...]
    scale = lax.rsqrt(jnp.mean(mid * mid, axis=1, keepdims=True) + EPS)
    gained = grad * gain[...]
    terms[...] = (grad * mid * scale).astype(BF)
    result = (
        cotangent[...].astype(F32)
        + scale * gained
        - mid * scale**3 * jnp.mean(gained * mid, axis=1, keepdims=True)
    )
    grad_middle[...] = result
    proj = (keep[...] * result).astype(BF)
    for t in range(sent.shape[0]):
        sent[t] = proj


def token_grad_kernel(parts, tokens, grad_middle, gain, out):
    grad = total_of([parts[t] for t in range(parts.shape[0])])
    x = tokens[...].astype(F32)
    scale = lax.rsqrt(jnp.mean(x * x, axis=1, keepdims=True) + EPS)
    gained = grad * gain[...]
    out[...] = (
        grad_middle[...]
        + scale * gained
        - x * scale**3 * jnp.mean(gained * x, axis=1, keepdims=True)
    )


def output_kernel(parts, middle, keep, out):
    ffn = total_of([parts[t] for t in range(parts.shape[0])])
    out[...] = (middle[...] + keep[...] * ffn).astype(BF)


def load_halves(sizes, pieces, target, sems, base):
    slots = 2 * sizes[0] * sizes[1]
    rows = target.shape[0] // (2 * slots)
    copies = []
    for piece in pieces:
        for at in range(0, piece.shape[0], rows):
            n = len(copies)
            place = (n % slots * 2 + n // slots) * rows
            copy = pltpu.make_async_copy(
                piece.at[pl.ds(at, rows), :], target.at[pl.ds(place, rows), :], sems.at[base + n]
            )
            copy.start()
            copies.append(copy)
    return copies


def mlp_kernel(sizes, count, meta, x, g, gate_rows, *refs):
    pieces = refs[: 2 * count]
    hidden, grad_gate, grad_up, grad_x, ffn, w_g, w_u, w_d, sems = refs[2 * count :]
    slots = 2 * sizes[0] * sizes[1]
    copies = load_natural(meta, sizes, gate_rows, w_g, sems, 0)
    copies += load_halves(sizes, pieces[:count], w_u, sems, slots)
    late = load_halves(sizes, pieces[count:], w_d, sems, 3 * slots)
    for copy in copies:
        copy.wait()
    features, width = w_g.shape

    def columns(lanes, wait=()):
        gate = dot(x[...], w_g[:, lanes])
        up = dot(x[...], w_u[:, lanes])
        for copy in wait:
            copy.wait()
        grad = dot(g[...], w_d[:, lanes])
        sig = 1.0 / (1.0 + jnp.exp(-gate))
        silu = gate * sig
        hidden[:, lanes] = (silu * up).astype(BF)
        grad_gate[:, lanes] = (grad * up * sig * (1.0 + gate * (1.0 - sig))).astype(BF)
        grad_up[:, lanes] = (grad * silu).astype(BF)

    step = 256
    tail = width % step
    columns(pl.ds(width - tail, tail) if tail else pl.ds(width - step, step), late)

    def chunk(i, _):
        columns(pl.ds(pl.multiple_of(i * step, step), step))
        return 0

    lax.fori_loop(0, (width - 1) // step, chunk, 0)

    def back_rows(i, _):
        at = pl.ds(pl.multiple_of(i * step, step), step)
        total = dot(grad_gate[...], w_g[at, :], 1, 1) + dot(grad_up[...], w_u[at, :], 1, 1)
        grad_x[:, at] = total.astype(BF)
        ffn[:, at] = dot(hidden[...], w_d[at, :], 1, 1).astype(BF)
        return 0

    lax.fori_loop(0, features // step, back_rows, 0)


def mlp(meta, sizes, x, g, w_gate, w_up, w_down):
    rows, features = x.shape
    width = w_gate.shape[1]
    count = len(w_up)
    pieces = [w_gate, *w_up, *w_down]
    copies = 5 * 2 * sizes[0] * sizes[1]
    return call(
        functools.partial(mlp_kernel, sizes, count),
        "mlp",
        [((rows, width), BF)] * 3 + [((rows, features), BF)] * 2,
        [meta, x, g, *pieces],
        [SMEM] + [VMEM] * 2 + [ANY] * len(pieces),
        [*([pltpu.VMEM((features, width), BF)] * 3), pltpu.SemaphoreType.DMA((copies,))],
        12 * rows * features * width,
    )


def outer_kernel(meta, left, right, *refs):
    product = dot(left[...].T, right[...])
    if len(refs) == 2:
        product = product + refs[0][...].astype(F32)
    refs[-1][...] = product.astype(BF)


def outer(meta, sizes, left, right, half=None, natural=False, added=None):
    features = left.shape[1]
    if features // (2 * sizes[0] * sizes[1]) % HEAD_DIM:
        sizes_held = features if half is None else features // 2
        part = left if half is None else left[:, half * sizes_held : (half + 1) * sizes_held]
        product = dot(part, right, 0, 0)
        if natural:
            shape = (sizes[0], sizes[1], -1, right.shape[1])
            product = product.reshape(shape)
            for axis, name in enumerate(("far", "zh")):
                product = by_distance(product, axis, lax.axis_index(name))
            product = product.reshape(sizes_held, -1)
        return (product if added is None else product + added.astype(F32)).astype(BF)
    slots = 2 * sizes[0] * sizes[1]
    rows, block, width = left.shape[0], features // slots, right.shape[1]
    count, start = (slots, 0) if half is None else (slots // 2, half * slots // 2)
    held = pl.BlockSpec((block, width), lambda i, m: (i, 0))
    natural_rows = pl.BlockSpec(
        (block, width), lambda i, m: (lax.rem(natural_slot(m, sizes, i), count), 0)
    )
    return pl.pallas_call(
        outer_kernel,
        out_shape=jax.ShapeDtypeStruct((count * block, width), BF),
        grid_spec=pltpu.PrefetchScalarGridSpec(
            num_scalar_prefetch=1,
            grid=(count,),
            in_specs=[
                pl.BlockSpec((rows, block), lambda i, m: (0, start + i)),
                pl.BlockSpec((rows, width), lambda i, m: (0, 0)),
            ]
            + ([] if added is None else [natural_rows if natural else held]),
            out_specs=natural_rows if natural else held,
        ),
        compiler_params=pltpu.CompilerParams(vmem_limit_bytes=48 << 20),
        cost_estimate=pl.CostEstimate(
            flops=2 * rows * count * block * width,
            bytes_accessed=2 * count * block * (rows + width),
            transcendentals=0,
        ),
        name="outer",
    )(meta, left, right, *([] if added is None else [added]))


def qkv_grad_kernel(count, grad_q, grad_kv, x, scale, *refs):
    pieces = refs[:count]
    out, terms, w, sems = refs[count:]
    for copy in load_pieces(pieces, w, sems, 0):
        copy.wait()
    q_width = grad_q.shape[1]
    step = 256

    def rows_of(i, _):
        at = pl.ds(pl.multiple_of(i * step, step), step)
        grad = dot(grad_q[...], w[at, :q_width], 1, 1) + dot(
            grad_kv[...], w[at, q_width : q_width + 2 * HEAD_DIM], 1, 1
        )
        out[:, at] = grad.astype(BF)
        terms[:, at] = (grad * x[:, at].astype(F32) * scale[...]).astype(BF)
        return 0

    lax.fori_loop(0, w.shape[0] // step, rows_of, 0)


def qkv_grad(grad_q, grad_kv, tokens_all, scale_all, pieces):
    rows, features = tokens_all.shape
    width = pieces[0].shape[1]
    return call(
        functools.partial(qkv_grad_kernel, len(pieces)),
        "qkv_grad",
        [((rows, features), BF)] * 2,
        [grad_q, grad_kv, tokens_all, scale_all, *pieces],
        [VMEM] * 4 + [ANY] * len(pieces),
        [pltpu.VMEM((features, width), BF), pltpu.SemaphoreType.DMA((len(pieces),))],
        2 * rows * features * width,
    )


def after(value, *done):
    return lax.optimization_barrier((value, done))[0]


def together(*values):
    return lax.optimization_barrier(values)


def swap(block, axes, distance):
    size = lax.axis_size(axes)
    return lax.ppermute(block, axes, [(i, i ^ distance) for i in range(size)])


def by_distance(array, axis, index):
    size = array.shape[axis]
    bit = 1
    while bit < size:
        shape = array.shape[:axis] + (size // (2 * bit), 2, bit) + array.shape[axis + 1 :]
        pairs = array.reshape(shape)
        flipped = jnp.flip(pairs, axis + 1)
        array = jnp.where((index & bit) != 0, flipped, pairs).reshape(array.shape)
        bit *= 2
    return array


def halves(array):
    half = array.shape[1] // 2
    return array[:, :half], array[:, half:]


def to_team(pieces):
    return lax.all_to_all(pieces, TEAM, split_axis=0, concat_axis=0, tiled=True)


def sum_team(partial):
    team = lax.axis_size(TEAM)
    return to_team(partial.reshape(team, partial.shape[0] // team, partial.shape[1]))


def total_of(parts):
    total = parts[0].astype(F32)
    for i in range(1, len(parts)):
        total = total + parts[i].astype(F32)
    return total


def plane_direct(block):
    size = lax.axis_size("far") * lax.axis_size("zh")
    return [block] + [swap(block, ("far", "zh"), d) for d in range(1, size)]


def plane_first(block):
    near = [swap(block, "zh", d) for d in range(1, lax.axis_size("zh"))]
    far = [[swap(block, "far", d)] for d in range(1, lax.axis_size("far"))]
    return block, near, far


def plane_second(first, *done):
    block, near, far = first
    if done:
        near = after(near, *done)
    far = [f + [swap(b, "far", d + 1) for b in near] for d, f in enumerate(far)]
    return sum(far, [block] + near)


def both_cores(plane, joined=False):
    if joined or len(plane) > 4:
        plane = [jnp.concatenate(plane, axis=0)]
    return list(plane) + [swap(b, "core", 1) for b in plane]


def sum_axis(part, axis, *done):
    size = lax.axis_size(axis)
    rows = part.shape[0] // size
    got = [swap(part[d * rows : (d + 1) * rows], axis, d) for d in range(1, size)]
    if done:
        got = after(got, *done)
    return total_of([part[:rows]] + got).astype(BF)


SLOT = ("core", "far", "zh")


def spread(block):
    return lax.all_gather(block, SLOT, axis=0, tiled=True)


def gather_back(partial):
    return lax.psum_scatter(partial, ("far", "zh"), scatter_dimension=0, tiled=True)


def to_owner(part):
    team = lax.axis_size(TEAM)
    return to_team(part.reshape(team, part.shape[0] // team, part.shape[1]))


def wide(pieces):
    return pieces.transpose(1, 0, 2).reshape(pieces.shape[1], -1).astype(F32)


def turn(values, cosine, sine):
    half = HEAD_DIM // 2
    other = jnp.concatenate([values[:, half:], values[:, :half]], axis=1)
    return values * cosine + other * sine


def to_slots(array):
    sizes = [lax.axis_size(a) for a in AXES]
    rows, width = array.shape
    grid = array.reshape(rows, *sizes[:4], width // (sizes[0] * sizes[1] * sizes[2] * sizes[3]))
    for axis in (0, 2, 3):
        grid = by_distance(grid, axis + 1, lax.axis_index(AXES[axis]))
    return grid.transpose(0, 3, 1, 4, 2, 5).reshape(rows, width)


def from_slots(array):
    far, x, core, zh, zl = [lax.axis_size(a) for a in AXES]
    rows, width = array.shape
    grid = array.reshape(rows, core, far, zh, x, width // (core * far * zh * x))
    grid = grid.transpose(0, 2, 4, 1, 3, 5)
    for axis in (0, 2, 3):
        grid = by_distance(grid, axis + 1, lax.axis_index(AXES[axis]))
    return grid.reshape(rows, width)


def per_device(
    tokens,
    segment_ids,
    layer_skip,
    attn_gain,
    w_query,
    w_key,
    w_value,
    w_output,
    mlp_gain,
    w_gate,
    w_up,
    w_down,
    cotangent,
):
    far_n, x_n, core_n, zh_n, zl_n = [lax.axis_size(a) for a in AXES]
    far, x, core, zh, zl = [lax.axis_index(a) for a in AXES]
    team = x_n * zl_n
    rows = tokens.shape[0]
    tile = team * rows
    run = zl_n * rows
    docs = layer_skip.shape[0]
    part = HEADS * HEAD_DIM // team
    ff = w_gate.shape[1] // team
    width = attn_gain.shape[0]
    features = tokens.shape[1]

    ids = rows // width
    doc_index = lax.iota(jnp.int32, docs)
    skipped = jnp.sum(
        jnp.where(segment_ids[:, None] == doc_index[None, :], layer_skip[None, :], 0), axis=1
    )
    keep = (1 - skipped).astype(F32)[:, None]
    small = jnp.concatenate(
        [segment_ids.astype(BF).reshape(width, ids), attn_gain[:, None], mlp_gain[:, None]], axis=1
    )
    small = jnp.pad(small, ((0, 0), (0, HEAD_DIM - ids - 2)))
    small = jnp.concatenate([small] * team, axis=1)
    first_rows = to_team(pack(team, [w_query, w_key, w_value, small, w_output.T, w_gate]))
    first_rows = first_rows.reshape(-1, first_rows.shape[2])
    qkv_width = part + 3 * HEAD_DIM
    qkv_plane = plane_first(first_rows[:, :qkv_width])
    out_rows = first_rows[:, qkv_width : qkv_width + part]
    gate_rows = first_rows[:, qkv_width + part :]

    last_rows = pack(team, [w_up, w_down.T])
    tokens_own, tokens_sent = slots_and_copies(tokens, keep, False, team)
    cot_own, cot_sent = slots_and_copies(cotangent, keep, True, team)
    tokens_all = to_team(after(tokens_sent, first_rows)).reshape(tile, features)

    local = lax.iota(jnp.int32, tile)
    place = (local // run) * (core_n * zh_n * run) + local % run
    position = ((far * x_n * core_n + core) * zh_n + zh) * run + place
    rates = jnp.power(THETA, -lax.iota(jnp.int32, HEAD_DIM // 2).astype(F32) / (HEAD_DIM // 2))
    angles = position.astype(F32)[:, None] * rates[None, :]
    cosine = jnp.cos(angles)
    sine = jnp.sin(angles)
    cosine = jnp.concatenate([cosine, cosine], axis=1)
    sine = jnp.concatenate([-sine, sine], axis=1)

    qkv_plane, last_rows, cot_sent, tokens_all = together(
        qkv_plane, last_rows, cot_sent, tokens_all
    )
    w_out = spread(after(out_rows, qkv_plane))
    w_qkv = both_cores(plane_second(qkv_plane))
    tokens_all, w_qkv, cosine, sine = together(tokens_all, w_qkv, cosine, sine)
    last_rows = to_team(after(last_rows, tokens_all)).reshape(-1, last_rows.shape[2])

    normed_one, scale_all, q, kv, small_all = project(tokens_all, cosine, sine, w_qkv, ids)
    kv_plane = plane_first(kv)
    w_g = spread(after(gate_rows, kv))
    gain_one = small_all[ids : ids + 1]
    gain_two = small_all[ids + 1 : ids + 2]
    doc_starts = jnp.sum(
        (small_all[None, :ids] < doc_index.astype(F32)[:, None, None]).astype(F32), axis=(1, 2)
    ).astype(jnp.int32)
    query_seg = jnp.sum((position[:, None] >= doc_starts[None, 1:]).astype(jnp.int32), axis=1)
    query_start = jnp.sum(
        jnp.where(query_seg[:, None] == doc_index[None, :], doc_starts[None, :], 0), axis=1
    )
    low = (far * x_n * core_n + core) * zh_n + zh
    first_start = jnp.max(jnp.where(doc_starts <= low * run, doc_starts, 0))
    meta = jnp.concatenate([jnp.stack([far, core, zh, low, first_start // run]), doc_starts])
    sizes = (far_n, zh_n)
    tables = (
        cosine,
        sine,
        position[None, :],
        query_start[None, :],
        position[:, None],
        lax.iota(jnp.int32, tile)[:, None],
    )
    up_rows, down_rows = last_rows[:, :ff], last_rows[:, ff:]
    kv_plane, meta, tables = together(kv_plane, meta, tables)
    kv_plane = plane_second(kv_plane)
    kv_plane, w_out, up_rows, down_rows = together(kv_plane, w_out, up_rows, down_rows)
    grad_ffn = to_team(after(cot_sent, up_rows))
    kv = both_cores(kv_plane)
    low_rows = up_rows.shape[0] // 2
    up_a = plane_first(up_rows[:low_rows])
    attn, query, log_total = attention_forward(meta, docs, sizes, q, tables, kv)
    attn, grad_ffn, up_a = together(attn, grad_ffn, up_a)
    up_b = plane_first(after(up_rows[low_rows:], attn))
    grad_ffn = grad_ffn.reshape(tile, features)

    proj = call(
        functools.partial(proj_kernel, sizes),
        "proj",
        [((tile, features), BF)],
        [meta, attn, w_out],
        [SMEM, VMEM, ANY],
        [pltpu.VMEM(w_out.shape, BF), pltpu.SemaphoreType.DMA((2 * far_n * zh_n,))],
    )[0]
    down_a = plane_first(after(down_rows[:low_rows], attn))
    proj = sum_team(proj)
    up_a = plane_second(up_a)
    proj, up_a, up_b, down_a, w_g = together(proj, up_a, up_b, down_a, w_g)
    down_b = plane_first(after(down_rows[low_rows:], proj))
    middle, normed_sent = call(
        middle_kernel,
        "middle",
        [((rows, features), F32), ((team, rows, features), BF)],
        [proj, tokens_own, keep, gain_two],
    )
    normed_two = to_team(normed_sent)
    w_u = both_cores(up_a, True) + both_cores(plane_second(up_b), True)
    down_a = both_cores(plane_second(down_a), True)
    w_d = down_a + both_cores(plane_second(down_b), True)
    normed_two, w_u, w_d = together(normed_two, w_u, w_d)
    normed_two = normed_two.reshape(tile, features)

    hidden, grad_gate_act, grad_up_act, grad_two, ffn = mlp(
        meta, sizes, normed_two, grad_ffn, w_g, w_u, w_d
    )
    grad_two_parts = sum_team(grad_two)
    other_down = swap(outer(meta, sizes, grad_ffn, hidden, 1, True), "core", 1)
    other_gate = swap(outer(meta, sizes, normed_two, grad_gate_act, 1), "core", 1)
    other_up = swap(outer(meta, sizes, normed_two, grad_up_act, 1), "core", 1)
    grad_down = gather_back(outer(meta, sizes, grad_ffn, hidden, 0, True, other_down))
    gate_core = outer(meta, sizes, normed_two, grad_gate_act, 0, False, other_gate)
    up_core = outer(meta, sizes, normed_two, grad_up_act, 0, False, other_up)
    grad_two_parts, gate_core = together(grad_two_parts, gate_core)
    grad_middle, grad_proj_sent, terms_two = call(
        middle_grad_kernel,
        "middle_grad",
        [((rows, features), F32), ((team, rows, features), BF), ((rows, features), BF)],
        [grad_two_parts, middle, cot_own, keep, gain_two],
    )
    grad_proj = to_team(grad_proj_sent)
    gate_far = sum_axis(gate_core, "far", grad_proj_sent)
    grad_proj, up_core, gate_far = together(grad_proj, up_core, gate_far)
    grad_proj = grad_proj.reshape(tile, features)
    ffn = sum_team(after(ffn, grad_proj))
    grad_query, grad_kv = attention_backward(
        meta, docs, sizes, query, attn, grad_proj, w_out, log_total, tables, kv
    )
    gate_zh = sum_axis(gate_far, "zh", grad_kv)
    up_far = sum_axis(up_core, "far", grad_kv)
    grad_query, grad_kv, ffn, gate_zh, up_far, grad_down = together(
        grad_query, grad_kv, ffn, gate_zh, up_far, grad_down
    )
    half = grad_kv.shape[0] // 2
    other_kv = swap(grad_kv[half:], "core", 1)
    grad_query = after(grad_query, other_kv)
    attn_late = after(attn, other_kv)
    grad_kv = grad_kv[:half].astype(F32) + other_kv.astype(F32)
    grad_kv_parts = [grad_kv[:tile]] + [
        swap(grad_kv[d * tile : (d + 1) * tile].astype(BF), ("far", "zh"), d)
        for d in range(1, far_n * zh_n)
    ]
    output = to_natural(
        call(output_kernel, "output", [((rows, features), BF)], [ffn, middle, keep])[0]
    )
    other_q = jnp.concatenate(
        [
            outer(meta, sizes, normed_one, grad_query, half=1),
            outer(meta, sizes, grad_proj, attn_late, half=1),
        ],
        axis=1,
    )
    other_q = swap(other_q, "core", 1)
    own_q = jnp.concatenate(
        [
            outer(meta, sizes, normed_one, grad_query, half=0),
            outer(meta, sizes, grad_proj, attn_late, half=0),
        ],
        axis=1,
    )
    q_core = (own_q.astype(F32) + other_q.astype(F32)).astype(BF)
    grad_kv_parts, q_core = together(grad_kv_parts, q_core)
    q_far = sum_axis(q_core, "far")
    up_zh = sum_axis(after(up_far, grad_kv_parts), "zh")
    grad_kv_sum = total_of(grad_kv_parts)
    grad_key = turn(grad_kv_sum[:, :HEAD_DIM].astype(BF).astype(F32), cosine, -sine).astype(BF)
    grad_kv_tok = jnp.concatenate([grad_key, grad_kv_sum[:, HEAD_DIM:].astype(BF)], axis=1)
    grad_one, terms_one = qkv_grad(grad_query, grad_kv_tok, tokens_all, scale_all, w_qkv)
    grad_one = sum_team(grad_one)

    lanes = lax.broadcasted_iota(jnp.int32, (tile + rows, HEAD_DIM), 1)
    which = lax.broadcasted_iota(jnp.int32, (tile + rows, HEAD_DIM), 0) // tile
    pick = (lanes == which).astype(BF)
    terms = jnp.concatenate([terms_one, terms_two], axis=0)
    other_small, own_small = [
        jnp.concatenate(
            [
                outer(meta, sizes, normed_one, grad_kv_tok, half=i),
                outer(meta, sizes, terms, pick, half=i),
            ],
            axis=1,
        )
        for i in (1, 0)
    ]
    other_small = swap(other_small, "core", 1)
    small_core = (own_small.astype(F32) + other_small.astype(F32)).astype(BF)
    grad_one, small_core, q_far, up_zh = together(grad_one, small_core, q_far, up_zh)
    q_zh = sum_axis(q_far, "zh")
    rows_held = small_core.shape[0] // (far_n * zh_n)
    small_sum = total_of(
        [small_core[:rows_held]]
        + [
            swap(small_core[d * rows_held : (d + 1) * rows_held], ("far", "zh"), d)
            for d in range(1, far_n * zh_n)
        ]
    ).astype(BF)
    merged = to_owner(jnp.concatenate([grad_down, gate_zh, up_zh], axis=1))
    grad_down, grad_gate, grad_up = (
        merged[:, :, :ff], merged[:, :, ff : 2 * ff], merged[:, :, 2 * ff :]
    )
    grad_tokens = to_natural(
        call(
            token_grad_kernel,
            "token_grad",
            [((rows, features), F32)],
            [grad_one, tokens_own, grad_middle, gain_one],
        )[0]
    )
    finished = [wide(grad_gate), wide(grad_up), wide(grad_down).T]
    grad_w = jnp.concatenate([q_zh, small_sum], axis=1)
    grad_w, finished, output, grad_tokens = together(grad_w, finished, output, grad_tokens)
    grad_w = to_owner(grad_w)
    grad_out = grad_w[:, :, part : 2 * part]
    grad_w = jnp.concatenate([grad_w[:, :, :part], grad_w[:, :, 2 * part :]], axis=2)
    gains = total_of(grad_w[:, :, part + 2 * HEAD_DIM :])
    return (
        output,
        grad_tokens,
        gains[:, 0],
        wide(grad_w[:, :, :part]),
        wide(grad_w[:, :, part : part + HEAD_DIM]),
        wide(grad_w[:, :, part + HEAD_DIM : part + 2 * HEAD_DIM]),
        wide(grad_out).T,
        gains[:, 1],
        *finished,
    )


def solution(mesh):
    blk, uly = mesh.shape["blk"], mesh.shape["uly"]
    grid = Mesh(mesh.devices.reshape(blk // 4, 2, 2, uly // 2, 2), AXES)
    rows = P(AXES, None)
    cols = P(None, AXES)
    flat = P(AXES)
    return jax.shard_map(
        per_device,
        mesh=grid,
        in_specs=(
            rows, flat, P(), flat, rows, rows, rows, cols, flat, rows, rows, cols, rows,
        ),
        out_specs=(rows, rows, flat, rows, rows, rows, cols, flat, rows, rows, cols),
        check_vma=False,
    )
```

```python
import functools

import jax
import jax.numpy as jnp
from jax import lax
from jax.experimental import pallas as pl
from jax.experimental.pallas import tpu as pltpu
from jax.sharding import Mesh
from jax.sharding import PartitionSpec as P

HEADS = 16
KV_HEADS = 4
HEAD_DIM = 128
SHARE = HEADS // KV_HEADS

EPS = 1e-05
THETA = 10000.0
LOG2E = 1.4426950408889634
SCALE = HEAD_DIM ** (-0.5)
FAR = 1e30

AXES = ("far", "x", "core", "zh", "zl")
TEAM = ("x", "zl")

BF = jnp.bfloat16
F32 = jnp.float32


def dot(left, right, left_dim=1, right_dim=0):
    return lax.dot_general(
        left, right, (((left_dim,), (right_dim,)), ((), ())), preferred_element_type=F32
    )


def turned(values, cosine, sine):
    return values * cosine + pltpu.roll(values, HEAD_DIM // 2, axis=1) * sine


def visible(kpos, qpos, qstart):
    return (kpos <= qpos) & (kpos >= qstart)


def is_mixed(starts, base, run):
    mixed = False
    for start in starts:
        inside = (start > base) & (start < base + run)
        mixed = inside if mixed is False else (mixed | inside)
    return mixed


def run_row(meta, sizes, number, run):
    far_n, zh_n = sizes
    far, core, zh = (meta[i] for i in range(3))
    zh_r = lax.rem(number, zh_n)
    core_r = lax.rem(number // zh_n, 2)
    x_r = lax.rem(number // (2 * zh_n), 2)
    far_r = number // (4 * zh_n)
    slot = ((core_r ^ core) * far_n + (far_r ^ far)) * zh_n + (zh_r ^ zh)
    return pl.multiple_of((slot * 2 + x_r) * run, run)


def natural_slot(meta, sizes, i):
    far_n, zh_n = sizes
    far, core, zh = (meta[k] for k in range(3))
    zh_i = i % zh_n if isinstance(i, int) else lax.rem(i, zh_n)
    far_i = i // zh_n % far_n if isinstance(i, int) else lax.rem(i // zh_n, far_n)
    core_i = i // (zh_n * far_n)
    return ((core_i ^ core) * far_n + (far_i ^ far)) * zh_n + (zh_i ^ zh)


def pair_rows(meta, sizes, i, run):
    return [pl.ds(run_row(meta, sizes, 2 * i + n, run), run) for n in range(2)]


def forward_kernel(
    docs, sizes, run, count, meta, q, cosine, sine, qpos, qstart, kown, klocal, *refs
):
    low = meta[3]
    high = low + 2 * sizes[1]
    first = meta[4]
    starts = [meta[5 + d] for d in range(docs)]
    factor = SCALE * LOG2E
    tile = 2 * run
    out, q_rot, lse, kv, sems, top, total, acc = refs[count:]
    copies = load_pieces(refs[:count], kv, sems, 0)
    for copy in copies:
        copy.wait()

    heads = range(SHARE)
    for h in heads:
        lanes = slice(h * HEAD_DIM, (h + 1) * HEAD_DIM)
        q_rot[:, lanes] = turned(q[:, lanes], cosine[...], sine[...]).astype(BF)
    top[...] = jnp.full_like(top, -FAR)
    total[...] = jnp.zeros_like(total)
    acc[...] = jnp.zeros_like(acc)

    def fold(i, masked):
        base = i * tile
        rows = pair_rows(meta, sizes, i, run)
        keys = jnp.concatenate([kv[r, :HEAD_DIM] for r in rows], axis=0)
        values = jnp.concatenate([kv[r, HEAD_DIM:] for r in rows], axis=0).T
        seen = (qstart[...] <= base) & (qpos[...] >= base + tile - 1)
        if masked:
            allowed = visible(klocal[...] + base, qpos[...], qstart[...])
        for h in heads:
            lanes = slice(h * HEAD_DIM, (h + 1) * HEAD_DIM)
            raw = dot(keys, q_rot[:, lanes], 1, 1)
            before = top[h : h + 1, :]
            if masked:
                raw = jnp.where(allowed, raw, -FAR)
                peak = jnp.maximum(before, jnp.max(raw, axis=0, keepdims=True))
                level = jnp.where(peak > -0.5 * FAR, peak * factor, FAR)
            else:
                new = jnp.max(raw, axis=0, keepdims=True)
                peak = jnp.maximum(before, jnp.where(seen, new, -FAR))
                level = jnp.where(seen, peak * factor, FAR)
            weights = jnp.exp2(raw * factor - level)
            fade = jnp.exp2((before - peak) * factor)
            top[h : h + 1, :] = peak
            total[h : h + 1, :] = total[h : h + 1, :] * fade + jnp.sum(
                weights, axis=0, keepdims=True
            )
            acc[h] = acc[h] * fade + dot(values, weights.astype(BF))

    def step(i, _):
        mixed = is_mixed(starts, i * tile, tile) | (i == low // 2) | (i == high // 2)

        @pl.when(mixed)
        def _():
            fold(i, True)

        @pl.when(jnp.logical_not(mixed))
        def _():
            fold(i, False)

        return 0

    lax.fori_loop(first // 2, high // 2 + 1, step, 0)
    for h in heads:
        lanes = slice(h * HEAD_DIM, (h + 1) * HEAD_DIM)
        out[:, lanes] = (acc[h] / total[h : h + 1, :]).T.astype(BF)
    lse[...] = top[...] * factor + jnp.log2(total[...])


def load_natural(meta, sizes, source, target, sems, base):
    slots = 2 * sizes[0] * sizes[1]
    block = source.shape[0] // slots
    copies = []
    for i in range(slots):
        away = pl.ds(pl.multiple_of(natural_slot(meta, sizes, i) * block, block), block)
        copy = pltpu.make_async_copy(
            source.at[away, :], target.at[pl.ds(i * block, block), :], sems.at[base + i]
        )
        copy.start()
        copies.append(copy)
    return copies


def proj_kernel(sizes, meta, attn, w_out, proj, held, sems):
    for copy in load_natural(meta, sizes, w_out, held, sems, 0):
        copy.wait()
    for at in range(0, held.shape[0], 256):
        proj[:, at : at + 256] = dot(attn[...], held[at : at + 256, :], 1, 1).astype(BF)


def backward_kernel(
    docs, sizes, run, count, meta, q, o, g_proj, w_out, lse, cosine, sine, qpos, qstart, kown, klocal, *refs
):
    low = meta[3]
    high = low + 2 * sizes[1]
    first = meta[4]
    starts = [meta[5 + d] for d in range(docs)]
    factor = SCALE * LOG2E
    tile = 2 * run
    grad_q, grad_kv, kv, held, sems, dqt, delta, g = refs[count:]
    copies = load_pieces(refs[:count], kv, sems, 0)
    for copy in load_natural(meta, sizes, w_out, held, sems, count):
        copy.wait()
    total = dot(g_proj[...], held[...])
    for copy in copies:
        copy.wait()
    g[...] = total.astype(BF)
    dqt[...] = jnp.zeros_like(dqt)
    grad_kv[...] = jnp.zeros_like(grad_kv)

    def prepare(h, _):
        lanes = pl.ds(pl.multiple_of(h * HEAD_DIM, HEAD_DIM), HEAD_DIM)
        both = o[:, lanes].astype(F32) * g[:, lanes].astype(F32)
        delta[pl.ds(h, 1), :] = jnp.sum(both.T, axis=0, keepdims=True)
        return 0

    lax.fori_loop(0, SHARE, prepare, 0)

    def key_step(i, masked):
        base = i * tile
        rows = pair_rows(meta, sizes, i, run)
        k_tile = jnp.concatenate([kv[r, :HEAD_DIM] for r in rows], axis=0)
        v_tile = jnp.concatenate([kv[r, HEAD_DIM:] for r in rows], axis=0)
        kt = k_tile.T
        seen = (qstart[...] <= base) & (qpos[...] >= base + tile - 1)
        if masked:
            allowed = visible(klocal[...] + base, qpos[...], qstart[...])
        grad_k = jnp.zeros((tile, HEAD_DIM), F32)
        grad_v = jnp.zeros((tile, HEAD_DIM), F32)
        for h in range(SHARE):
            lanes = slice(h * HEAD_DIM, (h + 1) * HEAD_DIM)
            q_head = q[:, lanes]
            g_head = g[:, lanes]
            raw = dot(k_tile, q_head, 1, 1) * factor
            level = lse[h : h + 1, :]
            if masked:
                probs = jnp.where(allowed, jnp.exp2(raw - level), 0.0)
            else:
                probs = jnp.exp2(raw - jnp.where(seen, level, FAR))
            slopes = dot(v_tile, g_head, 1, 1)
            grads = (probs * (slopes - delta[h : h + 1, :])).astype(BF)
            grad_v = grad_v + dot(probs.astype(BF), g_head)
            grad_k = grad_k + dot(grads, q_head)
            dqt[h] = dqt[h] + dot(kt, grads)
        for n, at in enumerate(rows):
            part = slice(n * run, (n + 1) * run)
            grad_kv[at, :HEAD_DIM] = (grad_k[part] * SCALE).astype(BF)
            grad_kv[at, HEAD_DIM:] = grad_v[part].astype(BF)

    def step(i, _):
        mixed = is_mixed(starts, i * tile, tile) | (i == low // 2) | (i == high // 2)

        @pl.when(mixed)
        def _():
            key_step(i, True)

        @pl.when(jnp.logical_not(mixed))
        def _():
            key_step(i, False)

        return 0

    lax.fori_loop(first // 2, high // 2 + 1, step, 0)

    def finish(h, _):
        lanes = pl.ds(pl.multiple_of(h * HEAD_DIM, HEAD_DIM), HEAD_DIM)
        rotated = (dqt[h] * SCALE).T.astype(BF).astype(F32)
        grad_q[:, lanes] = turned(rotated, cosine[...], -sine[...]).astype(BF)
        return 0

    lax.fori_loop(0, SHARE, finish, 0)


SMEM = pl.BlockSpec(memory_space=pltpu.SMEM)
VMEM = pl.BlockSpec(memory_space=pltpu.VMEM)
ANY = pl.BlockSpec(memory_space=pl.ANY)


def attention_forward(meta, docs, sizes, q, tables, kv):
    tile = q.shape[0]
    run = tile // 2
    span = sum(a.shape[0] for a in kv)
    pairs = tile * span // 2 * SHARE
    return pl.pallas_call(
        functools.partial(forward_kernel, docs, sizes, run, len(kv)),
        out_shape=(
            jax.ShapeDtypeStruct(q.shape, BF),
            jax.ShapeDtypeStruct(q.shape, BF),
            jax.ShapeDtypeStruct((SHARE, tile), F32),
        ),
        in_specs=[SMEM] + [VMEM] * (1 + len(tables)) + [ANY] * len(kv),
        out_specs=(VMEM, VMEM, VMEM),
        scratch_shapes=[
            pltpu.VMEM((span, 2 * HEAD_DIM), BF),
            pltpu.SemaphoreType.DMA((len(kv),)),
            pltpu.VMEM((SHARE, tile), F32),
            pltpu.VMEM((SHARE, tile), F32),
            pltpu.VMEM((SHARE, HEAD_DIM, tile), F32),
        ],
        compiler_params=pltpu.CompilerParams(vmem_limit_bytes=56 << 20),
        cost_estimate=pl.CostEstimate(
            flops=pairs * HEAD_DIM * 4, bytes_accessed=4 << 20, transcendentals=pairs
        ),
        name="attention_forward",
    )(meta, q, *tables, *kv)


def attention_backward(meta, docs, sizes, q, o, g_proj, w_out, lse, tables, kv):
    tile = q.shape[0]
    run = tile // 2
    span = sum(a.shape[0] for a in kv)
    pairs = tile * span // 2 * SHARE
    return pl.pallas_call(
        functools.partial(backward_kernel, docs, sizes, run, len(kv)),
        out_shape=(
            jax.ShapeDtypeStruct(q.shape, BF),
            jax.ShapeDtypeStruct((span, 2 * HEAD_DIM), BF),
        ),
        in_specs=[SMEM, VMEM, VMEM, VMEM, ANY] + [VMEM] * (1 + len(tables)) + [ANY] * len(kv),
        out_specs=(VMEM, VMEM),
        scratch_shapes=[
            pltpu.VMEM((span, 2 * HEAD_DIM), BF),
            pltpu.VMEM(w_out.shape, BF),
            pltpu.SemaphoreType.DMA((len(kv) + 2 * sizes[0] * sizes[1],)),
            pltpu.VMEM((SHARE, HEAD_DIM, tile), F32),
            pltpu.VMEM((SHARE, tile), F32),
            pltpu.VMEM(q.shape, BF),
        ],
        compiler_params=pltpu.CompilerParams(vmem_limit_bytes=56 << 20),
        cost_estimate=pl.CostEstimate(
            flops=pairs * HEAD_DIM * 10, bytes_accessed=6 << 20, transcendentals=pairs
        ),
        name="attention_backward",
    )(meta, q, o, g_proj, w_out, lse, *tables, *kv)


def call(kernel, name, shapes, operands, specs=None, scratch=(), flops=1 << 20):
    nbytes = sum(a.size * a.dtype.itemsize for a in operands)
    return pl.pallas_call(
        kernel,
        out_shape=tuple(jax.ShapeDtypeStruct(s, d) for s, d in shapes),
        in_specs=specs or [VMEM] * len(operands),
        out_specs=(VMEM,) * len(shapes),
        scratch_shapes=list(scratch),
        compiler_params=pltpu.CompilerParams(vmem_limit_bytes=56 << 20),
        cost_estimate=pl.CostEstimate(flops=flops, bytes_accessed=nbytes, transcendentals=0),
        name=name,
    )(*operands)


def load_pieces(pieces, target, sems, base):
    copies = []
    place = 0
    for i, piece in enumerate(pieces):
        rows = piece.shape[0]
        copy = pltpu.make_async_copy(piece, target.at[pl.ds(place, rows), :], sems.at[base + i])
        copy.start()
        copies.append(copy)
        place += rows
    return copies


def pack_kernel(team, count, *refs):
    out = refs[count]
    place = 0
    for shard in refs[:count]:
        part = shard.shape[1] // team
        for t in range(team):
            out[t, :, place : place + part] = shard[:, t * part : (t + 1) * part]
        place += part


def pack(team, shards):
    width = sum(s.shape[1] for s in shards) // team
    kernel = functools.partial(pack_kernel, team, len(shards))
    return call(kernel, "pack", [((team, shards[0].shape[0], width), BF)], shards)[0]


def slots_kernel(chunk, scaled, copies, order, array, keep, own, sent):
    width = array.shape[1]
    for j in range(width // chunk):
        if chunk < width:
            block = array[:, pl.ds(pl.multiple_of(order[j] * chunk, chunk), chunk)]
        else:
            block = array[...]
        lanes = pl.ds(j * chunk, chunk)
        own[:, lanes] = block
        if scaled:
            block = (block.astype(F32) * keep[...]).astype(BF)
        for t in range(copies):
            sent[t, :, lanes] = block


def slots_and_copies(array, keep, scaled, copies):
    chunk, order = slot_order(array.shape[1], True)
    if order is None:
        array, order = to_slots(array), jnp.zeros((1,), jnp.int32)
    kernel = functools.partial(slots_kernel, chunk, scaled, copies)
    shapes = [(array.shape, BF), ((copies,) + array.shape, BF)]
    return call(kernel, "to_slots", shapes, [order, array, keep], [SMEM, VMEM, VMEM])


def natural_kernel(chunk, order, array, out):
    for j in range(array.shape[1] // chunk):
        out[:, j * chunk : (j + 1) * chunk] = array[
            :, pl.ds(pl.multiple_of(order[j] * chunk, chunk), chunk)
        ]


def to_natural(array):
    chunk, order = slot_order(array.shape[1], False)
    if order is None:
        return from_slots(array)
    kernel = functools.partial(natural_kernel, chunk)
    return call(kernel, "from_slots", [(array.shape, array.dtype)], [order, array], [SMEM, VMEM])[0]


def slot_order(width, forward):
    far_n, x_n, core_n, zh_n, _ = [lax.axis_size(a) for a in AXES]
    far, _, core, zh, _ = [lax.axis_index(a) for a in AXES]
    count = far_n * x_n * core_n * zh_n
    chunk = width // count
    if chunk % HEAD_DIM:
        return width, None
    j = lax.iota(jnp.int32, count)
    if forward:
        c, f, z, x = j // (far_n * zh_n * x_n), j // (zh_n * x_n) % far_n, j // x_n % zh_n, j % x_n
        return chunk, (((f ^ far) * x_n + x) * core_n + (c ^ core)) * zh_n + (z ^ zh)
    f, x, c, z = j // (x_n * core_n * zh_n), j // (core_n * zh_n) % x_n, j // zh_n % core_n, j % zh_n
    return chunk, (((c ^ core) * far_n + (f ^ far)) * zh_n + (z ^ zh)) * x_n + x


def project_kernel(count, ids, x, cosine, sine, *refs):
    pieces = refs[:count]
    normed, scale, q, kv, small, w, sems = refs[count:]
    copies = load_pieces(pieces, w, sems, 0)
    rows = x.shape[0]
    features = x.shape[1]
    step = 128

    def squares(i, _):
        at = pl.ds(pl.multiple_of(i * step, step), step)
        block = x[at, :].astype(F32)
        scale[at, :] = lax.rsqrt(jnp.sum(block * block, axis=1, keepdims=True) / features + EPS)
        return 0

    lax.fori_loop(0, rows // step, squares, 0)
    for copy in copies:
        copy.wait()
    width = w.shape[1] - HEAD_DIM
    turned_small = w[:, width:].astype(F32).T
    small[...] = turned_small[: small.shape[0], :]
    gain = small[ids : ids + 1, :]

    def norm(i, _):
        at = pl.ds(pl.multiple_of(i * step, step), step)
        normed[at, :] = (x[at, :].astype(F32) * scale[at, :] * gain).astype(BF)
        return 0

    lax.fori_loop(0, rows // step, norm, 0)
    for at in range(0, width - 2 * HEAD_DIM, 256):
        q[:, at : at + 256] = dot(normed[...], w[:, at : at + 256])
    both = dot(normed[...], w[:, width - 2 * HEAD_DIM : width])
    kv[:, :HEAD_DIM] = turned(both[:, :HEAD_DIM], cosine[...], sine[...]).astype(BF)
    kv[:, HEAD_DIM:] = both[:, HEAD_DIM:].astype(BF)


def project(tokens_all, cosine, sine, pieces, ids):
    rows, features = tokens_all.shape
    width = pieces[0].shape[1]
    held = -(-(ids + 2) // 8) * 8
    return call(
        functools.partial(project_kernel, len(pieces), ids),
        "project",
        [
            ((rows, features), BF),
            ((rows, 1), F32),
            ((rows, width - 3 * HEAD_DIM), F32),
            ((rows, 2 * HEAD_DIM), BF),
            ((held, features), F32),
        ],
        [tokens_all, cosine, sine, *pieces],
        [VMEM] * 3 + [ANY] * len(pieces),
        [pltpu.VMEM((features, width), BF), pltpu.SemaphoreType.DMA((len(pieces),))],
        2 * rows * features * width,
    )


def middle_kernel(parts, tokens, keep, gain, middle, sent):
    proj = total_of([parts[t] for t in range(parts.shape[0])])
    mid = tokens[...].astype(F32) + keep[...] * proj
    scale = lax.rsqrt(jnp.mean(mid * mid, axis=1, keepdims=True) + EPS)
    middle[...] = mid
    normed = (mid * scale * gain[...]).astype(BF)
    for t in range(sent.shape[0]):
        sent[t] = normed


def middle_grad_kernel(parts, middle, cotangent, keep, gain, grad_middle, sent, terms):
    grad = total_of([parts[t] for t in range(parts.shape[0])])
    mid = middle[...]
    scale = lax.rsqrt(jnp.mean(mid * mid, axis=1, keepdims=True) + EPS)
    gained = grad * gain[...]
    terms[...] = (grad * mid * scale).astype(BF)
    result = (
        cotangent[...].astype(F32)
        + scale * gained
        - mid * scale**3 * jnp.mean(gained * mid, axis=1, keepdims=True)
    )
    grad_middle[...] = result
    proj = (keep[...] * result).astype(BF)
    for t in range(sent.shape[0]):
        sent[t] = proj


def token_grad_kernel(parts, tokens, grad_middle, gain, out):
    grad = total_of([parts[t] for t in range(parts.shape[0])])
    x = tokens[...].astype(F32)
    scale = lax.rsqrt(jnp.mean(x * x, axis=1, keepdims=True) + EPS)
    gained = grad * gain[...]
    out[...] = (
        grad_middle[...]
        + scale * gained
        - x * scale**3 * jnp.mean(gained * x, axis=1, keepdims=True)
    )


def output_kernel(parts, middle, keep, out):
    ffn = total_of([parts[t] for t in range(parts.shape[0])])
    out[...] = (middle[...] + keep[...] * ffn).astype(BF)


def load_halves(sizes, pieces, target, sems, base):
    slots = 2 * sizes[0] * sizes[1]
    rows = target.shape[0] // (2 * slots)
    copies = []
    for piece in pieces:
        for at in range(0, piece.shape[0], rows):
            n = len(copies)
            place = (n % slots * 2 + n // slots) * rows
            copy = pltpu.make_async_copy(
                piece.at[pl.ds(at, rows), :], target.at[pl.ds(place, rows), :], sems.at[base + n]
            )
            copy.start()
            copies.append(copy)
    return copies


def mlp_kernel(sizes, count, meta, x, g, gate_rows, *refs):
    pieces = refs[: 2 * count]
    hidden, grad_gate, grad_up, grad_x, ffn, w_g, w_u, w_d, sems = refs[2 * count :]
    slots = 2 * sizes[0] * sizes[1]
    copies = load_natural(meta, sizes, gate_rows, w_g, sems, 0)
    copies += load_halves(sizes, pieces[:count], w_u, sems, slots)
    late = load_halves(sizes, pieces[count:], w_d, sems, 3 * slots)
    for copy in copies:
        copy.wait()
    features, width = w_g.shape

    def columns(lanes, wait=()):
        gate = dot(x[...], w_g[:, lanes])
        up = dot(x[...], w_u[:, lanes])
        for copy in wait:
            copy.wait()
        grad = dot(g[...], w_d[:, lanes])
        sig = 1.0 / (1.0 + jnp.exp(-gate))
        silu = gate * sig
        hidden[:, lanes] = (silu * up).astype(BF)
        grad_gate[:, lanes] = (grad * up * sig * (1.0 + gate * (1.0 - sig))).astype(BF)
        grad_up[:, lanes] = (grad * silu).astype(BF)

    step = 256
    tail = width % step
    columns(pl.ds(width - tail, tail) if tail else pl.ds(width - step, step), late)

    def chunk(i, _):
        columns(pl.ds(pl.multiple_of(i * step, step), step))
        return 0

    lax.fori_loop(0, (width - 1) // step, chunk, 0)

    def back_rows(i, _):
        at = pl.ds(pl.multiple_of(i * step, step), step)
        total = dot(grad_gate[...], w_g[at, :], 1, 1) + dot(grad_up[...], w_u[at, :], 1, 1)
        grad_x[:, at] = total.astype(BF)
        ffn[:, at] = dot(hidden[...], w_d[at, :], 1, 1).astype(BF)
        return 0

    lax.fori_loop(0, features // step, back_rows, 0)


def mlp(meta, sizes, x, g, w_gate, w_up, w_down):
    rows, features = x.shape
    width = w_gate.shape[1]
    count = len(w_up)
    pieces = [w_gate, *w_up, *w_down]
    copies = 5 * 2 * sizes[0] * sizes[1]
    return call(
        functools.partial(mlp_kernel, sizes, count),
        "mlp",
        [((rows, width), BF)] * 3 + [((rows, features), BF)] * 2,
        [meta, x, g, *pieces],
        [SMEM] + [VMEM] * 2 + [ANY] * len(pieces),
        [*([pltpu.VMEM((features, width), BF)] * 3), pltpu.SemaphoreType.DMA((copies,))],
        12 * rows * features * width,
    )


def outer_kernel(meta, left, right, *refs):
    product = dot(left[...].T, right[...])
    if len(refs) == 2:
        product = product + refs[0][...].astype(F32)
    refs[-1][...] = product.astype(BF)


def outer(meta, sizes, left, right, half=None, natural=False, added=None):
    features = left.shape[1]
    if features // (2 * sizes[0] * sizes[1]) % HEAD_DIM:
        sizes_held = features if half is None else features // 2
        part = left if half is None else left[:, half * sizes_held : (half + 1) * sizes_held]
        product = dot(part, right, 0, 0)
        if natural:
            shape = (sizes[0], sizes[1], -1, right.shape[1])
            product = product.reshape(shape)
            for axis, name in enumerate(("far", "zh")):
                product = by_distance(product, axis, lax.axis_index(name))
            product = product.reshape(sizes_held, -1)
        return (product if added is None else product + added.astype(F32)).astype(BF)
    slots = 2 * sizes[0] * sizes[1]
    rows, block, width = left.shape[0], features // slots, right.shape[1]
    count, start = (slots, 0) if half is None else (slots // 2, half * slots // 2)
    held = pl.BlockSpec((block, width), lambda i, m: (i, 0))
    natural_rows = pl.BlockSpec(
        (block, width), lambda i, m: (lax.rem(natural_slot(m, sizes, i), count), 0)
    )
    return pl.pallas_call(
        outer_kernel,
        out_shape=jax.ShapeDtypeStruct((count * block, width), BF),
        grid_spec=pltpu.PrefetchScalarGridSpec(
            num_scalar_prefetch=1,
            grid=(count,),
            in_specs=[
                pl.BlockSpec((rows, block), lambda i, m: (0, start + i)),
                pl.BlockSpec((rows, width), lambda i, m: (0, 0)),
            ]
            + ([] if added is None else [natural_rows if natural else held]),
            out_specs=natural_rows if natural else held,
        ),
        compiler_params=pltpu.CompilerParams(vmem_limit_bytes=48 << 20),
        cost_estimate=pl.CostEstimate(
            flops=2 * rows * count * block * width,
            bytes_accessed=2 * count * block * (rows + width),
            transcendentals=0,
        ),
        name="outer",
    )(meta, left, right, *([] if added is None else [added]))


def qkv_grad_kernel(count, grad_q, grad_kv, x, scale, *refs):
    pieces = refs[:count]
    out, terms, w, sems = refs[count:]
    for copy in load_pieces(pieces, w, sems, 0):
        copy.wait()
    q_width = grad_q.shape[1]
    step = 256

    def rows_of(i, _):
        at = pl.ds(pl.multiple_of(i * step, step), step)
        grad = dot(grad_q[...], w[at, :q_width], 1, 1) + dot(
            grad_kv[...], w[at, q_width : q_width + 2 * HEAD_DIM], 1, 1
        )
        out[:, at] = grad.astype(BF)
        terms[:, at] = (grad * x[:, at].astype(F32) * scale[...]).astype(BF)
        return 0

    lax.fori_loop(0, w.shape[0] // step, rows_of, 0)


def qkv_grad(grad_q, grad_kv, tokens_all, scale_all, pieces):
    rows, features = tokens_all.shape
    width = pieces[0].shape[1]
    return call(
        functools.partial(qkv_grad_kernel, len(pieces)),
        "qkv_grad",
        [((rows, features), BF)] * 2,
        [grad_q, grad_kv, tokens_all, scale_all, *pieces],
        [VMEM] * 4 + [ANY] * len(pieces),
        [pltpu.VMEM((features, width), BF), pltpu.SemaphoreType.DMA((len(pieces),))],
        2 * rows * features * width,
    )


def after(value, *done):
    return lax.optimization_barrier((value, done))[0]


def together(*values):
    return lax.optimization_barrier(values)


def swap(block, axes, distance):
    size = lax.axis_size(axes)
    return lax.ppermute(block, axes, [(i, i ^ distance) for i in range(size)])


def by_distance(array, axis, index):
    size = array.shape[axis]
    bit = 1
    while bit < size:
        shape = array.shape[:axis] + (size // (2 * bit), 2, bit) + array.shape[axis + 1 :]
        pairs = array.reshape(shape)
        flipped = jnp.flip(pairs, axis + 1)
        array = jnp.where((index & bit) != 0, flipped, pairs).reshape(array.shape)
        bit *= 2
    return array


def halves(array):
    half = array.shape[1] // 2
    return array[:, :half], array[:, half:]


def to_team(pieces):
    return lax.all_to_all(pieces, TEAM, split_axis=0, concat_axis=0, tiled=True)


def sum_team(partial):
    team = lax.axis_size(TEAM)
    return to_team(partial.reshape(team, partial.shape[0] // team, partial.shape[1]))


def total_of(parts):
    total = parts[0].astype(F32)
    for i in range(1, len(parts)):
        total = total + parts[i].astype(F32)
    return total


def plane_direct(block):
    size = lax.axis_size("far") * lax.axis_size("zh")
    return [block] + [swap(block, ("far", "zh"), d) for d in range(1, size)]


def plane_first(block):
    near = [swap(block, "zh", d) for d in range(1, lax.axis_size("zh"))]
    far = [[swap(block, "far", d)] for d in range(1, lax.axis_size("far"))]
    return block, near, far


def plane_second(first, *done):
    block, near, far = first
    if done:
        near = after(near, *done)
    far = [f + [swap(b, "far", d + 1) for b in near] for d, f in enumerate(far)]
    return sum(far, [block] + near)


def both_cores(plane, joined=False):
    if joined or len(plane) > 4:
        plane = [jnp.concatenate(plane, axis=0)]
    return list(plane) + [swap(b, "core", 1) for b in plane]


def sum_axis(part, axis, *done):
    size = lax.axis_size(axis)
    rows = part.shape[0] // size
    got = [swap(part[d * rows : (d + 1) * rows], axis, d) for d in range(1, size)]
    if done:
        got = after(got, *done)
    return total_of([part[:rows]] + got).astype(BF)


SLOT = ("core", "far", "zh")


def spread(block):
    return lax.all_gather(block, SLOT, axis=0, tiled=True)


def gather_back(partial):
    return lax.psum_scatter(partial, ("far", "zh"), scatter_dimension=0, tiled=True)


def to_owner(part):
    team = lax.axis_size(TEAM)
    return to_team(part.reshape(team, part.shape[0] // team, part.shape[1]))


def wide(pieces):
    return pieces.transpose(1, 0, 2).reshape(pieces.shape[1], -1).astype(F32)


def turn(values, cosine, sine):
    half = HEAD_DIM // 2
    other = jnp.concatenate([values[:, half:], values[:, :half]], axis=1)
    return values * cosine + other * sine


def to_slots(array):
    sizes = [lax.axis_size(a) for a in AXES]
    rows, width = array.shape
    grid = array.reshape(rows, *sizes[:4], width // (sizes[0] * sizes[1] * sizes[2] * sizes[3]))
    for axis in (0, 2, 3):
        grid = by_distance(grid, axis + 1, lax.axis_index(AXES[axis]))
    return grid.transpose(0, 3, 1, 4, 2, 5).reshape(rows, width)


def from_slots(array):
    far, x, core, zh, zl = [lax.axis_size(a) for a in AXES]
    rows, width = array.shape
    grid = array.reshape(rows, core, far, zh, x, width // (core * far * zh * x))
    grid = grid.transpose(0, 2, 4, 1, 3, 5)
    for axis in (0, 2, 3):
        grid = by_distance(grid, axis + 1, lax.axis_index(AXES[axis]))
    return grid.reshape(rows, width)


def per_device(
    tokens,
    segment_ids,
    layer_skip,
    attn_gain,
    w_query,
    w_key,
    w_value,
    w_output,
    mlp_gain,
    w_gate,
    w_up,
    w_down,
    cotangent,
):
    far_n, x_n, core_n, zh_n, zl_n = [lax.axis_size(a) for a in AXES]
    far, x, core, zh, zl = [lax.axis_index(a) for a in AXES]
    team = x_n * zl_n
    rows = tokens.shape[0]
    tile = team * rows
    run = zl_n * rows
    docs = layer_skip.shape[0]
    part = HEADS * HEAD_DIM // team
    ff = w_gate.shape[1] // team
    width = attn_gain.shape[0]
    features = tokens.shape[1]

    ids = rows // width
    doc_index = lax.iota(jnp.int32, docs)
    skipped = jnp.sum(
        jnp.where(segment_ids[:, None] == doc_index[None, :], layer_skip[None, :], 0), axis=1
    )
    keep = (1 - skipped).astype(F32)[:, None]
    small = jnp.concatenate(
        [segment_ids.astype(BF).reshape(width, ids), attn_gain[:, None], mlp_gain[:, None]], axis=1
    )
    small = jnp.pad(small, ((0, 0), (0, HEAD_DIM - ids - 2)))
    small = jnp.concatenate([small] * team, axis=1)
    first_rows = to_team(pack(team, [w_query, w_key, w_value, small, w_output.T, w_gate]))
    first_rows = first_rows.reshape(-1, first_rows.shape[2])
    qkv_width = part + 3 * HEAD_DIM
    qkv_plane = plane_first(first_rows[:, :qkv_width])
    out_rows = first_rows[:, qkv_width : qkv_width + part]
    gate_rows = first_rows[:, qkv_width + part :]

    last_rows = pack(team, [w_up, w_down.T])
    tokens_own, tokens_sent = slots_and_copies(tokens, keep, False, team)
    cot_own, cot_sent = slots_and_copies(cotangent, keep, True, team)
    tokens_all = to_team(after(tokens_sent, first_rows)).reshape(tile, features)

    local = lax.iota(jnp.int32, tile)
    place = (local // run) * (core_n * zh_n * run) + local % run
    position = ((far * x_n * core_n + core) * zh_n + zh) * run + place
    rates = jnp.power(THETA, -lax.iota(jnp.int32, HEAD_DIM // 2).astype(F32) / (HEAD_DIM // 2))
    angles = position.astype(F32)[:, None] * rates[None, :]
    cosine = jnp.cos(angles)
    sine = jnp.sin(angles)
    cosine = jnp.concatenate([cosine, cosine], axis=1)
    sine = jnp.concatenate([-sine, sine], axis=1)

    qkv_plane, last_rows, cot_sent, tokens_all = together(
        qkv_plane, last_rows, cot_sent, tokens_all
    )
    w_out = spread(after(out_rows, qkv_plane))
    w_qkv = both_cores(plane_second(qkv_plane))
    tokens_all, w_qkv, cosine, sine = together(tokens_all, w_qkv, cosine, sine)
    last_rows = to_team(after(last_rows, tokens_all)).reshape(-1, last_rows.shape[2])

    normed_one, scale_all, q, kv, small_all = project(tokens_all, cosine, sine, w_qkv, ids)
    kv_plane = plane_first(kv)
    w_g = spread(after(gate_rows, kv))
    gain_one = small_all[ids : ids + 1]
    gain_two = small_all[ids + 1 : ids + 2]
    doc_starts = jnp.sum(
        (small_all[None, :ids] < doc_index.astype(F32)[:, None, None]).astype(F32), axis=(1, 2)
    ).astype(jnp.int32)
    query_seg = jnp.sum((position[:, None] >= doc_starts[None, 1:]).astype(jnp.int32), axis=1)
    query_start = jnp.sum(
        jnp.where(query_seg[:, None] == doc_index[None, :], doc_starts[None, :], 0), axis=1
    )
    low = (far * x_n * core_n + core) * zh_n + zh
    first_start = jnp.max(jnp.where(doc_starts <= low * run, doc_starts, 0))
    meta = jnp.concatenate([jnp.stack([far, core, zh, low, first_start // run]), doc_starts])
    sizes = (far_n, zh_n)
    tables = (
        cosine,
        sine,
        position[None, :],
        query_start[None, :],
        position[:, None],
        lax.iota(jnp.int32, tile)[:, None],
    )
    up_rows, down_rows = last_rows[:, :ff], last_rows[:, ff:]
    kv_plane, meta, tables = together(kv_plane, meta, tables)
    kv_plane = plane_second(kv_plane)
    kv_plane, w_out, up_rows, down_rows = together(kv_plane, w_out, up_rows, down_rows)
    grad_ffn = to_team(after(cot_sent, up_rows))
    kv = both_cores(kv_plane)
    low_rows = up_rows.shape[0] // 2
    up_a = plane_first(up_rows[:low_rows])
    attn, query, log_total = attention_forward(meta, docs, sizes, q, tables, kv)
    attn, grad_ffn, up_a = together(attn, grad_ffn, up_a)
    up_b = plane_first(after(up_rows[low_rows:], attn))
    grad_ffn = grad_ffn.reshape(tile, features)

    proj = call(
        functools.partial(proj_kernel, sizes),
        "proj",
        [((tile, features), BF)],
        [meta, attn, w_out],
        [SMEM, VMEM, ANY],
        [pltpu.VMEM(w_out.shape, BF), pltpu.SemaphoreType.DMA((2 * far_n * zh_n,))],
    )[0]
    down_a = plane_first(after(down_rows[:low_rows], attn))
    proj = sum_team(proj)
    up_a = plane_second(up_a)
    proj, up_a, up_b, down_a, w_g = together(proj, up_a, up_b, down_a, w_g)
    down_b = plane_first(after(down_rows[low_rows:], proj))
    middle, normed_sent = call(
        middle_kernel,
        "middle",
        [((rows, features), F32), ((team, rows, features), BF)],
        [proj, tokens_own, keep, gain_two],
    )
    normed_two = to_team(normed_sent)
    w_u = both_cores(up_a, True) + both_cores(plane_second(up_b), True)
    down_a = both_cores(plane_second(down_a), True)
    w_d = down_a + both_cores(plane_second(down_b), True)
    normed_two, w_u, w_d = together(normed_two, w_u, w_d)
    normed_two = normed_two.reshape(tile, features)

    hidden, grad_gate_act, grad_up_act, grad_two, ffn = mlp(
        meta, sizes, normed_two, grad_ffn, w_g, w_u, w_d
    )
    grad_two_parts = sum_team(grad_two)
    other_down = swap(outer(meta, sizes, grad_ffn, hidden, 1, True), "core", 1)
    other_gate = swap(outer(meta, sizes, normed_two, grad_gate_act, 1), "core", 1)
    other_up = swap(outer(meta, sizes, normed_two, grad_up_act, 1), "core", 1)
    grad_down = gather_back(outer(meta, sizes, grad_ffn, hidden, 0, True, other_down))
    gate_core = outer(meta, sizes, normed_two, grad_gate_act, 0, False, other_gate)
    up_core = outer(meta, sizes, normed_two, grad_up_act, 0, False, other_up)
    grad_two_parts, gate_core = together(grad_two_parts, gate_core)
    grad_middle, grad_proj_sent, terms_two = call(
        middle_grad_kernel,
        "middle_grad",
        [((rows, features), F32), ((team, rows, features), BF), ((rows, features), BF)],
        [grad_two_parts, middle, cot_own, keep, gain_two],
    )
    grad_proj = to_team(grad_proj_sent)
    gate_far = sum_axis(gate_core, "far", grad_proj_sent)
    grad_proj, up_core, gate_far = together(grad_proj, up_core, gate_far)
    grad_proj = grad_proj.reshape(tile, features)
    ffn = sum_team(after(ffn, grad_proj))
    grad_query, grad_kv = attention_backward(
        meta, docs, sizes, query, attn, grad_proj, w_out, log_total, tables, kv
    )
    gate_zh = sum_axis(gate_far, "zh", grad_kv)
    up_far = sum_axis(up_core, "far", grad_kv)
    grad_query, grad_kv, ffn, gate_zh, up_far, grad_down = together(
        grad_query, grad_kv, ffn, gate_zh, up_far, grad_down
    )
    half = grad_kv.shape[0] // 2
    other_kv = swap(grad_kv[half:], "core", 1)
    grad_query = after(grad_query, other_kv)
    attn_late = after(attn, other_kv)
    grad_kv = grad_kv[:half].astype(F32) + other_kv.astype(F32)
    grad_kv_parts = [grad_kv[:tile]] + [
        swap(grad_kv[d * tile : (d + 1) * tile].astype(BF), ("far", "zh"), d)
        for d in range(1, far_n * zh_n)
    ]
    output = to_natural(
        call(output_kernel, "output", [((rows, features), BF)], [ffn, middle, keep])[0]
    )
    other_q = jnp.concatenate(
        [
            outer(meta, sizes, normed_one, grad_query, half=1),
            outer(meta, sizes, grad_proj, attn_late, half=1),
        ],
        axis=1,
    )
    other_q = swap(other_q, "core", 1)
    own_q = jnp.concatenate(
        [
            outer(meta, sizes, normed_one, grad_query, half=0),
            outer(meta, sizes, grad_proj, attn_late, half=0),
        ],
        axis=1,
    )
    q_core = (own_q.astype(F32) + other_q.astype(F32)).astype(BF)
    grad_kv_parts, q_core = together(grad_kv_parts, q_core)
    q_far = sum_axis(q_core, "far")
    up_zh = sum_axis(after(up_far, grad_kv_parts), "zh")
    grad_kv_sum = total_of(grad_kv_parts)
    grad_key = turn(grad_kv_sum[:, :HEAD_DIM].astype(BF).astype(F32), cosine, -sine).astype(BF)
    grad_kv_tok = jnp.concatenate([grad_key, grad_kv_sum[:, HEAD_DIM:].astype(BF)], axis=1)
    grad_one, terms_one = qkv_grad(grad_query, grad_kv_tok, tokens_all, scale_all, w_qkv)
    grad_one = sum_team(grad_one)

    lanes = lax.broadcasted_iota(jnp.int32, (tile + rows, HEAD_DIM), 1)
    which = lax.broadcasted_iota(jnp.int32, (tile + rows, HEAD_DIM), 0) // tile
    pick = (lanes == which).astype(BF)
    terms = jnp.concatenate([terms_one, terms_two], axis=0)
    other_small, own_small = [
        jnp.concatenate(
            [
                outer(meta, sizes, normed_one, grad_kv_tok, half=i),
                outer(meta, sizes, terms, pick, half=i),
            ],
            axis=1,
        )
        for i in (1, 0)
    ]
    other_small = swap(other_small, "core", 1)
    small_core = (own_small.astype(F32) + other_small.astype(F32)).astype(BF)
    grad_one, small_core, q_far, up_zh = together(grad_one, small_core, q_far, up_zh)
    q_zh = sum_axis(q_far, "zh")
    small_sum = sum_axis(sum_axis(small_core, "far"), "zh")
    merged = to_owner(jnp.concatenate([grad_down, gate_zh, up_zh], axis=1))
    grad_down, grad_gate, grad_up = (
        merged[:, :, :ff], merged[:, :, ff : 2 * ff], merged[:, :, 2 * ff :]
    )
    grad_tokens = to_natural(
        call(
            token_grad_kernel,
            "token_grad",
            [((rows, features), F32)],
            [grad_one, tokens_own, grad_middle, gain_one],
        )[0]
    )
    finished = [wide(grad_gate), wide(grad_up), wide(grad_down).T]
    grad_w = jnp.concatenate([q_zh, small_sum], axis=1)
    grad_w, finished, output, grad_tokens = together(grad_w, finished, output, grad_tokens)
    grad_w = to_owner(grad_w)
    grad_out = grad_w[:, :, part : 2 * part]
    grad_w = jnp.concatenate([grad_w[:, :, :part], grad_w[:, :, 2 * part :]], axis=2)
    gains = total_of(grad_w[:, :, part + 2 * HEAD_DIM :])
    return (
        output,
        grad_tokens,
        gains[:, 0],
        wide(grad_w[:, :, :part]),
        wide(grad_w[:, :, part : part + HEAD_DIM]),
        wide(grad_w[:, :, part + HEAD_DIM : part + 2 * HEAD_DIM]),
        wide(grad_out).T,
        gains[:, 1],
        *finished,
    )


def solution(mesh):
    blk, uly = mesh.shape["blk"], mesh.shape["uly"]
    grid = Mesh(mesh.devices.reshape(blk // 4, 2, 2, uly // 2, 2), AXES)
    rows = P(AXES, None)
    cols = P(None, AXES)
    flat = P(AXES)
    return jax.shard_map(
        per_device,
        mesh=grid,
        in_specs=(
            rows, flat, P(), flat, rows, rows, rows, cols, flat, rows, rows, cols, rows,
        ),
        out_specs=(rows, rows, flat, rows, rows, rows, cols, flat, rows, rows, cols),
        check_vma=False,
    )
```
